512 devices in a mesh: dp: 8 (over y, core), expert: 64 (over x, z).
Axes of the slice: x: 4, y: 4, z: 16, core: 2. Of those that a mesh axis runs over, the one named last changes fastest.
Arguments:
- grad_out: bfloat16 [32768, 4096], P('expert', 'dp'), may hold values from -30 to 30
- hidden: bfloat16 [32768, 2, 1024], P('expert', None, 'dp'), may hold values from -24 to 24
- gate_prob: float32 [32768, 2], P('expert'), may hold values from 0.05 to 1
- expert_ids: int32 [32768, 2], P('expert'), may hold values from 0 to 63, all different within a row; in each aligned block of 512 rows (0 to 511, 512 to 1023, ...) at most 20 rows name the same one
- weights: bfloat16 [64, 1024, 4096], P('expert', None, 'dp'), may hold values from -0.1875 to 0.1875
Outputs:
- hidden_grad: bfloat16 [32768, 2, 1024], P('expert', None, 'dp')
- update: float32 [64, 1024, 4096], P('expert', None, 'dp')
The draws below stay inside these ranges and needn't reach their ends.
Inputs may be any that keep to these rules, and one draw needn't show every extreme that they name: `expert_ids`: among the 512 tokens of one index of expert, no expert is named by more than 20 choices, a bound that some block reaches; the 2 experts of a token differ.
All inputs are finite; a program needn't handle non-finite values.
Results may differ from the reference program's by a relative error of at most 0.019.
Values may be sent and summed in bfloat16 or wider, within the bound.
No kernel may reach another device: no remote copies, remote signals or barrier semaphores. Data moves between devices by JAX's collectives and lax.ppermute only.
A program may use at most 64 MiB of HBM per device.

```python
import math
import jax
import jax.numpy as jnp
import numpy as np
from jax import lax

D = 4096
F = 1024
TOPK = 2
TOK_DEV = 512
NEXP = 64
CAP = 20
TOKENS = 32768
N_DP = 8
N_EXPERT = 64


def draw_grad_out(key, part):
    key_noise = jax.random.fold_in(key, 11)
    key_scale = jax.random.fold_in(key, 12)
    column = jnp.arange(D, dtype=jnp.float32) / D
    spread = jnp.exp(jnp.log(3.0) * column + jnp.log(3.4) * jax.random.uniform(key_scale, (D,), jnp.float32))
    noise_part = jax.random.normal(key_noise, (TOKENS, D), jnp.float32)
    values = noise_part
    return jnp.clip(0.4 * values * spread[None, :], -30.0, 30.0).astype(jnp.bfloat16)


def draw_hidden(key, part):
    key_noise = jax.random.fold_in(key, 21)
    key_scale = jax.random.fold_in(key, 22)
    unit_scale = jnp.exp(jnp.log(10.0) * jax.random.uniform(key_scale, (F,), jnp.float32))
    noise_part = jax.random.normal(key_noise, (TOKENS, TOPK, F), jnp.float32)
    return jnp.clip(0.3 * noise_part * unit_scale, -24.0, 24.0).astype(jnp.bfloat16)


def steps_of(rng, dims, split, least, top_value):
    loudness, own = 1.0, jax.random.fold_in(rng, 6)
    for position, shards_of in split:
        steps = jnp.exp(jax.random.uniform(jax.random.fold_in(own, position), (shards_of,), jnp.float32, least / len(split), top_value / len(split)))
        loudness = loudness * jnp.repeat(steps, dims[position] // shards_of).reshape([-1 if axis == position else 1 for axis in range(len(dims))])
    return loudness


def routed_block(own_key, own, number, rows, count, top, most, skew):
    sequence = jax.random.permutation(own_key, count)
    crowded, common = portions_of(count, rows * top, most, skew, True), portions_of(count, rows * top, most, skew, False)
    places = jnp.arange(count)

    def named(lengths, rotation):
        used = int((lengths > 0).sum())
        fixed = max(1, used // 4)
        moved = fixed + (places - fixed + rotation * (used - fixed)) % max(1, count - fixed)
        return jnp.zeros((count,), jnp.int32).at[sequence[jnp.where(places < fixed, places, moved)]].set(jnp.asarray(lengths, jnp.int32))

    lengths = jnp.where(number % 4 == 0, named(crowded, number // 4), named(common, number - number // 4 - 1))
    mixed = jax.random.permutation(jax.random.fold_in(own, 3), count)
    donor, receiver = mixed[0:count // 2 * 2:2], mixed[1:count // 2 * 2:2]
    margin = jnp.minimum(lengths[donor] - 1, most - lengths[receiver]) // 2
    margin = jnp.where((donor == sequence[0]) | (receiver == sequence[0]) | (lengths[receiver] == 0), 0, jnp.maximum(margin, 0))
    moved = jax.random.randint(jax.random.fold_in(own, 4), (count // 2,), 0, 1 << 20) % (margin + 1)
    lengths = lengths.at[donor].add(-moved).at[receiver].add(moved)
    items = jnp.searchsorted(jnp.cumsum(lengths), jnp.arange(rows * top), side="right").astype(jnp.int32)
    listing = items.reshape(top, rows).T
    listing = listing[jax.random.permutation(jax.random.fold_in(own, 1), rows)]
    rotation = jax.random.randint(jax.random.fold_in(own, 2), (rows, 1), 0, top)
    return jnp.take_along_axis(listing, (jnp.arange(top)[None, :] + rotation) % top, axis=1)


def portions_of(count, total, bound, skew, full):
    loads = [(1 << 20) // math.isqrt(rank ** skew) + 1 for rank in range(1, count + 1)]
    largest = bound if full else min(bound, max(-(-total // count), total * loads[0] // sum(loads)))
    least = 1 if total - largest >= count - 1 else 0
    holding, surplus = [largest] + [least] * (count - 1), total - largest - least * (count - 1)
    while surplus > 0:
        free = [i for i in range(1, count) if holding[i] < largest] or [i for i in range(1, count) if holding[i] < bound]
        pool, left = sum([loads[i] for i in free]), surplus
        for i in free:
            addition = min(bound - holding[i], max(1, left * loads[i] // pool), surplus)
            holding[i] = holding[i] + addition
            surplus = surplus - addition
    return np.array(holding)


def noise(own_key, shape, scale, reach, split=(), held_as=jnp.bfloat16):
    loudness = steps_of(own_key, shape, split, -0.22, 0.18) if split else 1.0
    array = jax.random.normal(own_key, shape, jnp.float32) * scale * loudness
    return jnp.minimum(jnp.maximum(array, -reach), reach).astype(held_as)


def setup_inputs(seed: int = 0) -> dict:
    key_list = jax.random.split(jax.random.key(seed), 6)
    grad_out = draw_grad_out(jax.random.fold_in(key_list[5], 71), 0)
    hidden = draw_hidden(jax.random.fold_in(key_list[5], 71), 0)
    gate_prob = jnp.clip(0.05 + 0.95 * jax.random.uniform(key_list[2], (TOKENS, TOPK), jnp.float32) ** steps_of(key_list[2], (TOKENS, TOPK), ((0, 64),), -0.2, 0.2), 0.05, 1.0)
    expert_ids_keys = jax.random.split(jax.random.fold_in(key_list[3], 1), TOKENS // TOK_DEV)
    expert_ids_turns = jax.random.permutation(jax.random.fold_in(key_list[3], 3), TOKENS // TOK_DEV)
    expert_ids = jax.vmap(lambda own, number: routed_block(jax.random.fold_in(key_list[3], 2), own, number, TOK_DEV, NEXP, TOPK, CAP, 1))(expert_ids_keys, expert_ids_turns).reshape((TOKENS, TOPK))
    weights = noise(key_list[4], (NEXP, F, D), F ** -0.5, 0.1875, ((0, 64), (2, 8)))
    return {"grad_out": grad_out, "hidden": hidden, "gate_prob": gate_prob, "expert_ids": expert_ids, "weights": weights}


def slot_numbers(route_ids, capacity, expert_count):
    flat_ids = route_ids.reshape(-1)
    one_hot = (flat_ids[:, None] == jnp.arange(expert_count, dtype=jnp.int32)[None, :]).astype(jnp.int32)
    before = jnp.cumsum(one_hot, axis=0) - one_hot
    rank_in = lax.optimization_barrier(jnp.sum(before * one_hot, axis=1))
    return (flat_ids * capacity + rank_in).astype(jnp.int32)

def rounded(value):
    return lax.optimization_barrier(value.astype(jnp.bfloat16)).astype(jnp.float32)

def block_gram(matrix_b):
    width_part = D // N_DP
    gram_total = jnp.zeros((F, F), jnp.float32)
    for block_number in range(N_DP):
        column_piece = matrix_b[:, block_number * width_part:(block_number + 1) * width_part]
        gram_total = gram_total + rounded(jnp.dot(column_piece, column_piece.T, preferred_element_type=jnp.float32))
    return gram_total

def reference(grad_out, hidden, gate_prob, expert_ids, weights):
    pair_count = TOK_DEV * TOPK
    total_slots = NEXP * CAP
    width_part = D // N_DP
    source_ids = expert_ids.reshape(N_EXPERT, TOK_DEV, TOPK)
    slot_index = jax.vmap(lambda route_part: slot_numbers(route_part, CAP, NEXP))(source_ids)
    source_rows = jnp.arange(N_EXPERT, dtype=jnp.int32)[:, None]
    owner_table = jnp.full((N_EXPERT, total_slots), pair_count, jnp.int32)
    owner_table = owner_table.at[source_rows, slot_index].set(jnp.arange(pair_count, dtype=jnp.int32)[None, :])
    flat_hidden = hidden.reshape(N_EXPERT * pair_count, F)
    flat_prob = gate_prob.reshape(-1)

    def one_expert(packed):
        expert_number, weight_matrix = packed
        chosen = lax.dynamic_slice_in_dim(owner_table, (expert_number * CAP).astype(jnp.int32), CAP, 1)
        is_valid = chosen < pair_count
        safe_pair = jnp.where(is_valid, chosen, 0)
        global_pair = (source_rows * pair_count + safe_pair).reshape(-1).astype(jnp.int32)
        is_valid = is_valid.reshape(-1)
        token_rows = global_pair // TOPK
        grad_rows = jnp.where(is_valid[:, None], grad_out[token_rows], 0)
        prob_rows = jnp.where(is_valid, flat_prob[global_pair], 0.0)
        scaled = (prob_rows[:, None] * flat_hidden[global_pair].astype(jnp.float32)).astype(jnp.bfloat16)
        gradient = jnp.dot(scaled.T, grad_rows, preferred_element_type=jnp.float32)
        grad_bf16 = gradient.astype(jnp.bfloat16)
        back_total = jnp.zeros((total_slots, F), jnp.float32)
        for block_number in range(N_DP):
            column_start = block_number * width_part
            column_end = column_start + width_part
            block_term = jnp.dot(grad_rows[:, column_start:column_end], weight_matrix[:, column_start:column_end].T, preferred_element_type=jnp.float32)
            back_total = back_total + rounded(block_term)
        gram_first = block_gram(grad_bf16)
        norm_sq = jnp.sqrt(jnp.sum(gram_first * gram_first)) + 1e-06
        current = (grad_bf16.astype(jnp.float32) * lax.rsqrt(norm_sq)).astype(jnp.bfloat16)
        gram_now = (gram_first / norm_sq).astype(jnp.bfloat16)
        following = current.astype(jnp.float32)
        for sweep_number in range(2):
            if sweep_number > 0:
                gram_now = block_gram(current).astype(jnp.bfloat16)
            following = 1.5 * current.astype(jnp.float32) - 0.5 * jnp.dot(gram_now, current, preferred_element_type=jnp.float32)
            current = following.astype(jnp.bfloat16)
        return (back_total, following * D ** 0.5)
    slot_grads, update = lax.map(one_expert, (jnp.arange(NEXP, dtype=jnp.int32), weights))
    expert_flat = expert_ids.reshape(N_EXPERT, pair_count)
    slot_row = expert_flat * total_slots + source_rows * CAP + slot_index - expert_flat * CAP
    picked = slot_grads.reshape(NEXP * total_slots, F)[slot_row.reshape(-1).astype(jnp.int32)]
    hidden_grad = (flat_prob[:, None] * picked).astype(jnp.bfloat16).reshape(TOKENS, TOPK, F)
    return (hidden_grad, update)
```

```python
import jax
import jax.numpy as jnp
from jax import lax
from jax.experimental import pallas as pl
from jax.experimental.pallas import tpu as pltpu
from jax.sharding import Mesh, PartitionSpec as P

EXPERT = ("x", "z")
VMEM_LIMIT = 50 * 1024 * 1024
BF16 = jnp.bfloat16
F32 = jnp.float32


def full_spec():
    return pl.BlockSpec(memory_space=pltpu.VMEM)


def smem_spec():
    return pl.BlockSpec(memory_space=pltpu.SMEM)


def shift_y(value, step, size):
    return lax.ppermute(value, "y", [(i, (i + step) % size) for i in range(size)])


def swap_core(value):
    return lax.ppermute(value, "c", [(0, 1), (1, 0)])


def nt_dot(left, right):
    return lax.dot_general(left, right, (((1,), (1,)), ((), ())), preferred_element_type=F32)


def grad_kernel(spot_ref, own_ref, other_ref, rows_ref, gradb_ref, pack_own_ref, pack_other_ref, wide_ref):
    blocks = gradb_ref.shape[0] // 128
    y_size = blocks // 2
    for d in range(blocks):
        spot = spot_ref[d]

        @pl.when(spot < y_size)
        def _():
            wide_ref[:, d * 128 : (d + 1) * 128] = own_ref[spot]

        @pl.when(spot >= y_size)
        def _():
            wide_ref[:, d * 128 : (d + 1) * 128] = other_ref[spot - y_size]

    gradient = lax.dot_general(
        wide_ref[...], rows_ref[...], (((0,), (0,)), ((), ())), preferred_element_type=F32
    )
    gradb = gradient.astype(BF16)
    gradb_ref[...] = gradb
    gram = nt_dot(gradb, gradb).astype(BF16)
    half = blocks // 2
    for d in range(blocks):
        rows = slice(d * 128, (d + 1) * 128)
        pieces = []
        for k in range(half):
            j = (d + k) % blocks
            pieces.append(gram[rows, j * 128 : (j + 1) * 128])
        i = d % half
        top = i * 128 + (64 if d >= half else 0)
        pieces.append(gram[top : top + 64, (i + half) * 128 : (i + half + 1) * 128])
        spot = spot_ref[blocks + d]

        def put(ref, at):
            for k in range(half):
                ref[at, k * 128 : (k + 1) * 128, :] = pieces[k]
            ref[at, half * 128 : half * 128 + 64, :] = pieces[half]

        @pl.when(spot < y_size)
        def _():
            put(pack_own_ref, spot)

        @pl.when(spot >= y_size)
        def _():
            put(pack_other_ref, spot - y_size)


def back_kernel(spot_ref, rows_ref, weight_ref, own_ref, other_ref):
    blocks = weight_ref.shape[0] // 128
    y_size = blocks // 2
    term = nt_dot(rows_ref[...], weight_ref[...]).astype(BF16)
    for d in range(blocks):
        spot = spot_ref[blocks + d]
        piece = term[:, d * 128 : (d + 1) * 128]

        @pl.when(spot < y_size)
        def _():
            own_ref[spot] = piece

        @pl.when(spot >= y_size)
        def _():
            other_ref[spot - y_size] = piece


def ortho_kernel(width, spot_ref, own_ref, other_ref, gradb_ref, out_ref, gram_ref):
    blocks = gradb_ref.shape[0] // 128
    y_size = blocks // 2
    half = blocks // 2
    for d in range(blocks):
        spot = spot_ref[d]

        def place(ref, at):
            for k in range(half):
                j = (d + k) % blocks
                block = ref[at, k * 128 : (k + 1) * 128, :]
                gram_ref[d * 128 : (d + 1) * 128, j * 128 : (j + 1) * 128] = block
                if k > 0:
                    gram_ref[j * 128 : (j + 1) * 128, d * 128 : (d + 1) * 128] = block.T
            i = d % half
            top = i * 128 + (64 if d >= half else 0)
            gram_ref[top : top + 64, (i + half) * 128 : (i + half + 1) * 128] = ref[
                at, half * 128 : half * 128 + 64, :
            ]

        @pl.when(spot < y_size)
        def _():
            place(own_ref, spot)

        @pl.when(spot >= y_size)
        def _():
            place(other_ref, spot - y_size)

    for i in range(half):
        upper = gram_ref[i * 128 : (i + 1) * 128, (i + half) * 128 : (i + half + 1) * 128]
        gram_ref[(i + half) * 128 : (i + half + 1) * 128, i * 128 : (i + 1) * 128] = upper.T

    gram = gram_ref[...]
    wide = gram.astype(F32)
    norm_sq = jnp.sqrt(jnp.sum(wide * wide, keepdims=True)) + 1e-06
    inverse = 1.0 / norm_sq
    first = (gradb_ref[...].astype(F32) * lax.rsqrt(norm_sq)).astype(BF16)

    def apply(value):
        return jnp.dot(gram, value, preferred_element_type=F32) * inverse

    second = (1.5 * first.astype(F32) - 0.5 * apply(first)).astype(BF16)
    power_one = apply(second)
    power_two = apply(power_one.astype(BF16))
    power_three = apply(power_two.astype(BF16))
    total = 1.5 * second.astype(F32) - 0.5 * (2.25 * power_one - 1.5 * power_two + 0.25 * power_three)
    out_ref[0] = total * width**0.5


def call(kernel, outs, ins, scratch=()):
    return pl.pallas_call(
        kernel,
        out_shape=outs,
        in_specs=[smem_spec()] + [full_spec()] * (len(ins) - 1),
        out_specs=jax.tree.map(lambda _: full_spec(), outs),
        scratch_shapes=list(scratch),
        compiler_params=pltpu.CompilerParams(vmem_limit_bytes=VMEM_LIMIT),
    )(*ins)


def per_device(grad_out, hidden, gate_prob, expert_ids, weights):
    tokens, width_part = grad_out.shape
    top_count = expert_ids.shape[1]
    unit_part = hidden.shape[2]
    units = weights.shape[1]
    experts = lax.axis_size("x") * lax.axis_size("z")
    y_size = lax.axis_size("y")
    dp = y_size * 2
    width = width_part * dp
    capacity = 5 * tokens * top_count // (4 * experts)
    total_slots = experts * capacity
    pair_count = tokens * top_count
    y = lax.axis_index("y")
    c = lax.axis_index("c")
    block = jnp.arange(dp, dtype=jnp.int32)
    other_core = (block % 2) ^ c
    came_from = other_core * y_size + (y - block // 2) % y_size
    goes_to = other_core * y_size + (block // 2 - y) % y_size
    spots = jnp.concatenate([came_from, goes_to]).astype(jnp.int32)

    flat_ids = expert_ids.T.reshape(1, pair_count)
    named = (jnp.arange(experts, dtype=jnp.int32)[:, None] == flat_ids).astype(BF16)
    order = jnp.arange(pair_count, dtype=jnp.int32)
    earlier = (order[:, None] < order[None, :]).astype(BF16)
    before = jnp.dot(named, earlier, preferred_element_type=F32)
    rank_in = jnp.sum(before * named.astype(F32), axis=0, keepdims=True).astype(jnp.int32)
    slot_index = flat_ids * capacity + rank_in
    chosen = (jnp.arange(total_slots, dtype=jnp.int32)[:, None] == slot_index).astype(BF16)
    chosen_token = chosen[:, :tokens] + chosen[:, tokens:]

    scaled_part = (gate_prob[:, :, None] * hidden.astype(F32)).astype(BF16)
    scaled_part = scaled_part.transpose(1, 0, 2).reshape(pair_count, unit_part)
    send_scaled = jnp.dot(chosen, scaled_part, preferred_element_type=F32).astype(BF16)
    got_scaled = lax.all_to_all(
        send_scaled.reshape(experts, capacity, unit_part), EXPERT, split_axis=0, concat_axis=0, tiled=True
    ).reshape(total_slots, unit_part)

    send_grad = jnp.dot(chosen_token, grad_out, preferred_element_type=F32).astype(BF16)
    send_grad = (
        send_grad.reshape(experts, capacity, 2, width_part // 2)
        .transpose(0, 2, 1, 3)
        .reshape(experts, 2 * capacity, width_part // 2)
    )
    got_grad = lax.all_to_all(send_grad, EXPERT, split_axis=0, concat_axis=0, tiled=True)
    got_grad = (
        got_grad.reshape(experts, 2, capacity, width_part // 2)
        .transpose(0, 2, 1, 3)
        .reshape(total_slots, width_part)
    )

    gathered = jnp.stack([got_scaled] + [shift_y(got_scaled, k, y_size) for k in range(1, y_size)])
    gathered_other = swap_core(gathered)

    pack_rows = units // 2 + 64
    packs = jax.ShapeDtypeStruct((y_size, pack_rows, 128), BF16)
    grad_bf16, pack_own, pack_other = call(
        grad_kernel,
        (jax.ShapeDtypeStruct((units, width_part), BF16), packs, packs),
        (spots, gathered, gathered_other, got_grad),
        (pltpu.VMEM((total_slots, units), BF16),),
    )

    def reduce_dp(own, other):
        both = (own.astype(F32) + swap_core(other).astype(F32)).astype(BF16)
        parts = [both[0]] + [shift_y(both[k], k, y_size) for k in range(1, y_size)]
        total = parts[0].astype(F32)
        for part in parts[1:]:
            total = total + part.astype(F32)
        return total.astype(BF16)

    pack = reduce_dp(pack_own, pack_other)
    pack_all = jnp.stack([pack] + [shift_y(pack, k, y_size) for k in range(1, y_size)])
    pack_all_other = swap_core(pack_all)
    update = call(
        lambda *refs: ortho_kernel(width, *refs),
        jax.ShapeDtypeStruct((1, units, width_part), F32),
        (spots, pack_all, pack_all_other, grad_bf16),
        (pltpu.VMEM((units, units), BF16),),
    )

    terms = jax.ShapeDtypeStruct((y_size, total_slots, unit_part), BF16)
    term_own, term_other = call(back_kernel, (terms, terms), (spots, got_grad, weights[0]))
    summed = reduce_dp(term_own, term_other)
    returned = lax.all_to_all(
        summed.reshape(experts, capacity, unit_part), EXPERT, split_axis=0, concat_axis=0, tiled=True
    ).reshape(total_slots, unit_part)
    picked = lax.dot_general(chosen, returned, (((0,), (0,)), ((), ())), preferred_element_type=F32)
    picked = picked.reshape(top_count, tokens, unit_part).transpose(1, 0, 2)
    hidden_grad = (gate_prob[:, :, None] * picked).astype(BF16)
    return (hidden_grad, update)


def solution(mesh):
    dp, experts = mesh.devices.shape
    x_size = 4
    split = Mesh(
        mesh.devices.reshape(dp // 2, 2, x_size, experts // x_size), ("y", "c", "x", "z")
    )
    rows, cols = ("x", "z"), ("y", "c")
    in_specs = (P(rows, cols), P(rows, None, cols), P(rows, None), P(rows, None), P(rows, None, cols))
    out_specs = (P(rows, None, cols), P(rows, None, cols))
    return jax.shard_map(per_device, mesh=split, in_specs=in_specs, out_specs=out_specs, check_vma=False)
```

```python
import jax
import jax.numpy as jnp
from jax import lax
from jax.experimental import pallas as pl
from jax.experimental.pallas import tpu as pltpu
from jax.sharding import Mesh, PartitionSpec as P

EXPERT = ("x", "z")
VMEM_LIMIT = 24 * 1024 * 1024
BF16 = jnp.bfloat16
F32 = jnp.float32


def full_spec():
    return pl.BlockSpec(memory_space=pltpu.VMEM)


def smem_spec():
    return pl.BlockSpec(memory_space=pltpu.SMEM)


def shift_y(value, step, size):
    return lax.ppermute(value, "y", [(i, (i + step) % size) for i in range(size)])


def swap_core(value):
    return lax.ppermute(value, "c", [(0, 1), (1, 0)])


def nt_dot(left, right):
    return lax.dot_general(left, right, (((1,), (1,)), ((), ())), preferred_element_type=F32)


def one_hot(rows, index):
    return jnp.where(rows == index, 1.0, 0.0).astype(BF16)


def row_numbers(count):
    return lax.broadcasted_iota(jnp.int32, (count, 1), 0)


def first_send_kernel(main_ref, left_ref, scaled_ref, grad_ref, out_ref):
    experts = out_ref.shape[0]
    tokens, width_part = grad_ref.shape
    chosen = one_hot(row_numbers(experts * 16), main_ref[...])
    scaled = scaled_ref[...]
    part = jnp.dot(chosen, scaled, preferred_element_type=F32).astype(BF16)
    out_ref[:, 0:16, :] = part.reshape(experts, 16, 128)
    chosen_token = chosen[:, :tokens] + chosen[:, tokens:]
    rows = jnp.dot(chosen_token, grad_ref[...], preferred_element_type=F32).astype(BF16)
    blocks = width_part // 128
    for b in range(blocks):
        out_ref[:, 16 * (b + 1) : 16 * (b + 2), :] = rows[:, b * 128 : (b + 1) * 128].reshape(experts, 16, 128)
    left = one_hot(row_numbers(experts * 8), left_ref[...])
    part = jnp.dot(left, scaled, preferred_element_type=F32)
    out_ref[:, 16 * (blocks + 1) :, :] = part.reshape(experts, 8, 128).astype(BF16)


def second_send_kernel(index_ref, grad_ref, out_ref):
    experts = out_ref.shape[0]
    tokens, width_part = grad_ref.shape
    number = row_numbers(experts * 16)
    chosen = one_hot(number - number % 16 + number % 4, index_ref[...])
    chosen_token = chosen[:, :tokens] + chosen[:, tokens:]
    rows = jnp.dot(chosen_token, grad_ref[...], preferred_element_type=F32)
    column = (number % 16) // 4
    total = jnp.zeros((experts * 16, 128), F32)
    for b in range(width_part // 128):
        total = jnp.where(column == b, rows[:, b * 128 : (b + 1) * 128], total)
    out_ref[...] = total.astype(BF16).reshape(experts, 16, 128)


def unpack_kernel(got_ref, out_ref):
    experts, rows, _ = got_ref.shape
    out_ref[: experts * 16] = got_ref[:, 0:16, :].reshape(experts * 16, 128)
    tail = got_ref[:, rows - 8 :, :].astype(F32).reshape(experts * 8, 128).astype(BF16)
    number = row_numbers(experts * 4)
    source = lax.broadcasted_iota(jnp.int32, (1, experts * 8), 1)
    take = one_hot(number // 4 * 8 + number % 4, source)
    out_ref[experts * 16 :] = jnp.dot(take, tail, preferred_element_type=F32).astype(BF16)


def put_piece(spot, y_size, own_ref, other_ref, piece):
    @pl.when(spot < y_size)
    def _():
        own_ref[spot] = piece

    @pl.when(spot >= y_size)
    def _():
        other_ref[spot - y_size] = piece


def main_rows(got_ref, rows_ref):
    experts = got_ref.shape[0]
    for b in range(rows_ref.shape[1] // 128):
        rows_ref[: experts * 16, b * 128 : (b + 1) * 128] = got_ref[
            :, 16 * (b + 1) : 16 * (b + 2), :
        ].reshape(experts * 16, 128)


def back_main_kernel(spot_ref, got_ref, weight_ref, own_ref, other_ref, rows_ref):
    blocks = weight_ref.shape[0] // 128
    y_size = blocks // 2
    main_rows(got_ref, rows_ref)
    term = nt_dot(rows_ref[...], weight_ref[...]).astype(BF16)
    for d in range(blocks):
        put_piece(spot_ref[blocks + d], y_size, own_ref, other_ref, term[:, d * 128 : (d + 1) * 128])


def back_left_kernel(spot_ref, got_ref, weight_ref, own_ref, other_ref, rows_ref):
    blocks = weight_ref.shape[0] // 128
    y_size = blocks // 2
    experts = got_ref.shape[0]
    got = got_ref[...].reshape(experts * 16, 128)
    number = row_numbers(experts * 4)
    source = lax.broadcasted_iota(jnp.int32, (1, experts * 16), 1)
    for b in range(rows_ref.shape[1] // 128):
        take = one_hot(number // 4 * 16 + b * 4 + number % 4, source)
        rows_ref[:, b * 128 : (b + 1) * 128] = jnp.dot(take, got, preferred_element_type=F32).astype(BF16)
    term = nt_dot(rows_ref[...], weight_ref[...]).astype(BF16)
    for d in range(blocks):
        put_piece(spot_ref[blocks + d], y_size, own_ref, other_ref, term[:, d * 128 : (d + 1) * 128])


def grad_kernel(
    spot_ref, own_ref, other_ref, got_ref, left_ref, gradb_ref, pack_own_ref, pack_other_ref, wide_ref, rows_ref
):
    blocks = gradb_ref.shape[0] // 128
    y_size = blocks // 2
    main_rows(got_ref, rows_ref)
    rows_ref[got_ref.shape[0] * 16 :] = left_ref[...]
    for d in range(blocks):
        spot = spot_ref[d]

        @pl.when(spot < y_size)
        def _():
            wide_ref[:, d * 128 : (d + 1) * 128] = own_ref[spot]

        @pl.when(spot >= y_size)
        def _():
            wide_ref[:, d * 128 : (d + 1) * 128] = other_ref[spot - y_size]

    gradient = lax.dot_general(
        wide_ref[...], rows_ref[...], (((0,), (0,)), ((), ())), preferred_element_type=F32
    )
    gradb = gradient.astype(BF16)
    gradb_ref[...] = gradb
    gram = nt_dot(gradb, gradb).astype(BF16)
    half = blocks // 2
    for d in range(blocks):
        rows = slice(d * 128, (d + 1) * 128)
        pieces = []
        for k in range(half):
            j = (d + k) % blocks
            pieces.append(gram[rows, j * 128 : (j + 1) * 128])
        i = d % half
        top = i * 128 + (64 if d >= half else 0)
        pieces.append(gram[top : top + 64, (i + half) * 128 : (i + half + 1) * 128])
        spot = spot_ref[blocks + d]

        def put(ref, at):
            for k in range(half):
                ref[at, k * 128 : (k + 1) * 128, :] = pieces[k]
            ref[at, half * 128 : half * 128 + 64, :] = pieces[half]

        @pl.when(spot < y_size)
        def _():
            put(pack_own_ref, spot)

        @pl.when(spot >= y_size)
        def _():
            put(pack_other_ref, spot - y_size)


def ortho_kernel(width, spot_ref, own_ref, other_ref, gradb_ref, out_ref, gram_ref):
    blocks = gradb_ref.shape[0] // 128
    y_size = blocks // 2
    half = blocks // 2
    for d in range(blocks):
        spot = spot_ref[d]

        def place(ref, at):
            for k in range(half):
                j = (d + k) % blocks
                block = ref[at, k * 128 : (k + 1) * 128, :]
                gram_ref[d * 128 : (d + 1) * 128, j * 128 : (j + 1) * 128] = block
                if k > 0:
                    gram_ref[j * 128 : (j + 1) * 128, d * 128 : (d + 1) * 128] = block.T
            i = d % half
            top = i * 128 + (64 if d >= half else 0)
            gram_ref[top : top + 64, (i + half) * 128 : (i + half + 1) * 128] = ref[
                at, half * 128 : half * 128 + 64, :
            ]

        @pl.when(spot < y_size)
        def _():
            place(own_ref, spot)

        @pl.when(spot >= y_size)
        def _():
            place(other_ref, spot - y_size)

    for i in range(half):
        upper = gram_ref[i * 128 : (i + 1) * 128, (i + half) * 128 : (i + half + 1) * 128]
        gram_ref[(i + half) * 128 : (i + half + 1) * 128, i * 128 : (i + 1) * 128] = upper.T

    gram = gram_ref[...]
    wide = gram.astype(F32)
    norm_sq = jnp.sqrt(jnp.sum(wide * wide, keepdims=True)) + 1e-06
    inverse = 1.0 / norm_sq
    first = (gradb_ref[...].astype(F32) * lax.rsqrt(norm_sq)).astype(BF16)

    def apply(value):
        return jnp.dot(gram, value, preferred_element_type=F32) * inverse

    second = (1.5 * first.astype(F32) - 0.5 * apply(first)).astype(BF16)
    power_one = apply(second)
    power_two = apply(power_one.astype(BF16))
    power_three = apply(power_two.astype(BF16))
    total = 1.5 * second.astype(F32) - 0.5 * (2.25 * power_one - 1.5 * power_two + 0.25 * power_three)
    out_ref[0] = total * width**0.5


def call(kernel, outs, ins, scratch=(), scalars=1):
    return pl.pallas_call(
        kernel,
        out_shape=outs,
        in_specs=[smem_spec()] * scalars + [full_spec()] * (len(ins) - scalars),
        out_specs=jax.tree.map(lambda _: full_spec(), outs),
        scratch_shapes=list(scratch),
        compiler_params=pltpu.CompilerParams(vmem_limit_bytes=VMEM_LIMIT),
    )(*ins)


def per_device(grad_out, hidden, gate_prob, expert_ids, weights):
    tokens, width_part = grad_out.shape
    top_count = expert_ids.shape[1]
    unit_part = hidden.shape[2]
    units = weights.shape[1]
    experts = lax.axis_size("x") * lax.axis_size("z")
    y_size = lax.axis_size("y")
    dp = y_size * 2
    width = width_part * dp
    capacity = 5 * tokens * top_count // (4 * experts)
    total_slots = experts * capacity
    pair_count = tokens * top_count
    y = lax.axis_index("y")
    c = lax.axis_index("c")
    block = jnp.arange(dp, dtype=jnp.int32)
    other_core = (block % 2) ^ c
    came_from = other_core * y_size + (y - block // 2) % y_size
    goes_to = other_core * y_size + (block // 2 - y) % y_size
    spots = jnp.concatenate([came_from, goes_to]).astype(jnp.int32)

    flat_ids = expert_ids.T.reshape(1, pair_count)
    named = (jnp.arange(experts, dtype=jnp.int32)[:, None] == flat_ids).astype(BF16)
    order = jnp.arange(pair_count, dtype=jnp.int32)
    earlier = (order[:, None] < order[None, :]).astype(BF16)
    before = jnp.dot(named, earlier, preferred_element_type=F32)
    rank_in = jnp.sum(before * named.astype(F32), axis=0, keepdims=True).astype(jnp.int32)
    late = rank_in >= 16
    main_index = jnp.where(late, -1, flat_ids * 16 + rank_in)
    left_index = jnp.where(late, flat_ids * 8 + rank_in - 16, -1)
    second_index = jnp.where(late, flat_ids * 16 + rank_in - 16, -1)

    scaled_part = (gate_prob[:, :, None] * hidden.astype(F32)).astype(BF16)
    scaled_part = scaled_part.transpose(1, 0, 2).reshape(pair_count, unit_part)
    column_blocks = width_part // 128
    first_rows = 16 * (column_blocks + 1) + 8

    def exchange(value):
        return lax.all_to_all(value, EXPERT, split_axis=0, concat_axis=0, tiled=True)

    got_main = exchange(
        call(
            first_send_kernel,
            jax.ShapeDtypeStruct((experts, first_rows, 128), BF16),
            (main_index, left_index, scaled_part, grad_out),
            scalars=0,
        )
    )
    got_left = exchange(
        call(
            second_send_kernel,
            jax.ShapeDtypeStruct((experts, 4 * column_blocks, 128), BF16),
            (second_index, grad_out),
            scalars=0,
        )
    )

    got_scaled = call(
        unpack_kernel, jax.ShapeDtypeStruct((total_slots, unit_part), BF16), (got_main,), scalars=0
    )
    gathered = jnp.stack([got_scaled] + [shift_y(got_scaled, k, y_size) for k in range(1, y_size)])
    gathered_other = swap_core(gathered)

    def reduce_dp(own, other):
        both = (own.astype(F32) + swap_core(other).astype(F32)).astype(BF16)
        parts = [both[0]] + [shift_y(both[k], k, y_size) for k in range(1, y_size)]
        total = parts[0].astype(F32)
        for part in parts[1:]:
            total = total + part.astype(F32)
        return total.astype(BF16)

    def terms(count):
        return jax.ShapeDtypeStruct((y_size, count, unit_part), BF16)

    weight_part = weights[0]
    main_count = experts * 16
    left_count = total_slots - main_count
    main_own, main_other = call(
        back_main_kernel,
        (terms(main_count), terms(main_count)),
        (spots, got_main, weight_part),
        (pltpu.VMEM((main_count, width_part), BF16),),
    )
    summed_main = reduce_dp(main_own, main_other)
    left_own, left_other, left_rows = call(
        back_left_kernel,
        (terms(left_count), terms(left_count), jax.ShapeDtypeStruct((left_count, width_part), BF16)),
        (spots, got_left, weight_part),
    )
    summed_left = reduce_dp(left_own, left_other)
    returned = exchange(
        jnp.concatenate(
            [
                summed_main.reshape(experts, 16, unit_part),
                summed_left.reshape(experts, capacity - 16, unit_part),
            ],
            axis=1,
        )
    ).reshape(total_slots, unit_part)
    slot_index = flat_ids * capacity + rank_in
    chosen = (jnp.arange(total_slots, dtype=jnp.int32)[:, None] == slot_index).astype(BF16)
    picked = lax.dot_general(chosen, returned, (((0,), (0,)), ((), ())), preferred_element_type=F32)
    picked = picked.reshape(top_count, tokens, unit_part).transpose(1, 0, 2)
    hidden_grad = (gate_prob[:, :, None] * picked).astype(BF16)

    pack_rows = units // 2 + 64
    packs = jax.ShapeDtypeStruct((y_size, pack_rows, 128), BF16)
    grad_bf16, pack_own, pack_other = call(
        grad_kernel,
        (jax.ShapeDtypeStruct((units, width_part), BF16), packs, packs),
        (spots, gathered, gathered_other, got_main, left_rows),
        (pltpu.VMEM((total_slots, units), BF16), pltpu.VMEM((total_slots, width_part), BF16)),
    )
    pack = reduce_dp(pack_own, pack_other)
    pack_all = jnp.stack([pack] + [shift_y(pack, k, y_size) for k in range(1, y_size)])
    pack_all_other = swap_core(pack_all)
    update = call(
        lambda *refs: ortho_kernel(width, *refs),
        jax.ShapeDtypeStruct((1, units, width_part), F32),
        (spots, pack_all, pack_all_other, grad_bf16),
        (pltpu.VMEM((units, units), BF16),),
    )
    return (hidden_grad, update)


def solution(mesh):
    dp, experts = mesh.devices.shape
    x_size = 4
    split = Mesh(
        mesh.devices.reshape(dp // 2, 2, x_size, experts // x_size), ("y", "c", "x", "z")
    )
    rows, cols = ("x", "z"), ("y", "c")
    in_specs = (P(rows, cols), P(rows, None, cols), P(rows, None), P(rows, None), P(rows, None, cols))
    out_specs = (P(rows, None, cols), P(rows, None, cols))
    return jax.shard_map(per_device, mesh=split, in_specs=in_specs, out_specs=out_specs, check_vma=False)
```

```python
import jax
import jax.numpy as jnp
from jax import lax
from jax.experimental import pallas as pl
from jax.experimental.pallas import tpu as pltpu
from jax.sharding import Mesh, PartitionSpec as P

EXPERT = ("x", "z")
MIB = 1024 * 1024
BF16 = jnp.bfloat16
F32 = jnp.float32


def full_spec():
    return pl.BlockSpec(memory_space=pltpu.VMEM)


def smem_spec():
    return pl.BlockSpec(memory_space=pltpu.SMEM)


def shift_y(value, step, size):
    return lax.ppermute(value, "y", [(i, (i + step) % size) for i in range(size)])


def swap_core(value):
    return lax.ppermute(value, "c", [(0, 1), (1, 0)])


def nt_dot(left, right):
    return lax.dot_general(left, right, (((1,), (1,)), ((), ())), preferred_element_type=F32)


def one_hot(rows, index):
    return jnp.where(rows == index, 1.0, 0.0).astype(BF16)


def row_numbers(count):
    return lax.broadcasted_iota(jnp.int32, (count, 1), 0)


def send_kernel(main_ref, left_ref, scaled_ref, grad_ref, out_ref):
    experts, height, _ = out_ref.shape
    tokens, width_part = grad_ref.shape
    blocks = width_part // 128
    main = 16 * (blocks + 1)
    tail = height - main
    scaled = scaled_ref[...]
    grad = grad_ref[...]
    chosen = one_hot(row_numbers(experts * 16), main_ref[...])
    part = jnp.dot(chosen, scaled, preferred_element_type=F32).astype(BF16)
    out_ref[:, 0:16, :] = part.reshape(experts, 16, 128)
    chosen_token = chosen[:, :tokens] + chosen[:, tokens:]
    rows = jnp.dot(chosen_token, grad, preferred_element_type=F32).astype(BF16)
    for b in range(blocks):
        out_ref[:, 16 * (b + 1) : 16 * (b + 2), :] = rows[:, b * 128 : (b + 1) * 128].reshape(experts, 16, 128)
    expert = lax.broadcasted_iota(jnp.int32, (experts, tail, 1), 0)
    place = lax.broadcasted_iota(jnp.int32, (experts, tail, 1), 1)
    number = (expert * tail + (place & 3)).reshape(experts * tail, 1)
    kind = (place >> 2).reshape(experts * tail, 1)
    chosen = one_hot(number, left_ref[...])
    part = jnp.dot(chosen, scaled, preferred_element_type=F32)
    total = jnp.where(kind == 0, part, 0.0)
    chosen_token = chosen[:, :tokens] + chosen[:, tokens:]
    rows = jnp.dot(chosen_token, grad, preferred_element_type=F32)
    for b in range(blocks):
        total = jnp.where(kind == b + 1, rows[:, b * 128 : (b + 1) * 128], total)
    out_ref[:, main:, :] = total.reshape(experts, tail, 128).astype(BF16)


def tail_rows(tail, kind, experts, height):
    number = row_numbers(experts * 4)
    source = lax.broadcasted_iota(jnp.int32, (1, experts * height), 1)
    take = one_hot((number >> 2) * height + kind * 4 + (number & 3), source)
    return jnp.dot(take, tail, preferred_element_type=F32).astype(BF16)


def unpack_kernel(got_ref, out_ref):
    experts, height, _ = got_ref.shape
    main = (height // 16 - 1) * 16
    tail = got_ref[:, main:, :].astype(F32).reshape(experts * (height - main), 128).astype(BF16)
    left = tail_rows(tail, 0, experts, height - main)
    for k in range(out_ref.shape[0]):
        out_ref[k, : experts * 16] = got_ref[:, 0:16, :].reshape(experts * 16, 128)
        out_ref[k, experts * 16 :] = left


def put_piece(spot, y_size, own_ref, other_ref, piece):
    @pl.when(spot < y_size)
    def _():
        own_ref[spot] = piece

    @pl.when(spot >= y_size)
    def _():
        other_ref[spot - y_size] = piece


def back_kernel(spot_ref, got_ref, weight_ref, own_ref, other_ref, rows_ref):
    blocks = weight_ref.shape[0] // 128
    y_size = blocks // 2
    experts, height, _ = got_ref.shape
    columns = rows_ref.shape[1] // 128
    main = 16 * (columns + 1)
    tail = got_ref[:, main:, :].astype(F32).reshape(experts * (height - main), 128).astype(BF16)
    for b in range(columns):
        lanes = slice(b * 128, (b + 1) * 128)
        rows_ref[: experts * 16, lanes] = got_ref[:, 16 * (b + 1) : 16 * (b + 2), :].reshape(experts * 16, 128)
        rows_ref[experts * 16 :, lanes] = tail_rows(tail, b + 1, experts, height - main)
    term = nt_dot(rows_ref[...], weight_ref[...]).astype(BF16)
    for d in range(blocks):
        put_piece(spot_ref[d], y_size, own_ref, other_ref, term[:, d * 128 : (d + 1) * 128])


def add_kernel(own_ref, other_ref, after_ref, out_ref):
    out_ref[...] = (own_ref[...].astype(F32) + other_ref[...].astype(F32)).astype(BF16)


def gather_half(part_ref, rows_ref, wide_ref):
    for k in range(part_ref.shape[0]):
        wide_ref[:, k * 128 : (k + 1) * 128] = part_ref[k]
    return lax.dot_general(
        wide_ref[...], rows_ref[...], (((0,), (0,)), ((), ())), preferred_element_type=F32
    ).astype(BF16)


def grad_half_kernel(part_ref, rows_ref, half_ref, wide_ref):
    half_ref[...] = gather_half(part_ref, rows_ref, wide_ref).reshape(half_ref.shape)


def grad_kernel(spot_ref, own_half_ref, part_ref, rows_ref, gradb_ref, pack_own_ref, pack_other_ref, wide_ref):
    blocks = gradb_ref.shape[0]
    y_size = blocks // 2
    core = spot_ref[3 * blocks]
    other_half = gather_half(part_ref, rows_ref, wide_ref)
    for k in range(y_size):
        gradb_ref[2 * k + core] = own_half_ref[k]
        gradb_ref[2 * k + 1 - core] = other_half[k * 128 : (k + 1) * 128]
    gradb = gradb_ref[...].reshape(blocks * 128, gradb_ref.shape[2])
    gram = nt_dot(gradb, gradb).astype(BF16)
    half = blocks // 2
    for d in range(blocks):
        rows = slice(d * 128, (d + 1) * 128)
        pieces = []
        for k in range(half):
            j = (d + k) % blocks
            pieces.append(gram[rows, j * 128 : (j + 1) * 128])
        i = d % half
        top = i * 128 + (64 if d >= half else 0)
        pieces.append(gram[top : top + 64, (i + half) * 128 : (i + half + 1) * 128])
        spot = spot_ref[blocks + d]

        def put(ref, at):
            for k in range(half):
                ref[at, k * 128 : (k + 1) * 128, :] = pieces[k]
            ref[at, half * 128 : half * 128 + 64, :] = pieces[half]

        @pl.when(spot < y_size)
        def _():
            put(pack_own_ref, spot)

        @pl.when(spot >= y_size)
        def _():
            put(pack_other_ref, spot - y_size)


def ortho_kernel(width, spot_ref, own_ref, other_ref, gradb_ref, out_ref, gram_ref):
    blocks = gradb_ref.shape[0]
    y_size = blocks // 2
    half = blocks // 2
    for d in range(blocks):
        spot = spot_ref[2 * blocks + d]

        def place(ref, at):
            for k in range(half):
                j = (d + k) % blocks
                block = ref[at, k * 128 : (k + 1) * 128, :]
                gram_ref[d * 128 : (d + 1) * 128, j * 128 : (j + 1) * 128] = block
                if k > 0:
                    gram_ref[j * 128 : (j + 1) * 128, d * 128 : (d + 1) * 128] = block.T
            i = d % half
            top = i * 128 + (64 if d >= half else 0)
            gram_ref[top : top + 64, (i + half) * 128 : (i + half + 1) * 128] = ref[
                at, half * 128 : half * 128 + 64, :
            ]

        @pl.when(spot < y_size)
        def _():
            place(own_ref, spot)

        @pl.when(spot >= y_size)
        def _():
            place(other_ref, spot - y_size)

    for i in range(half):
        upper = gram_ref[i * 128 : (i + 1) * 128, (i + half) * 128 : (i + half + 1) * 128]
        gram_ref[(i + half) * 128 : (i + half + 1) * 128, i * 128 : (i + 1) * 128] = upper.T

    gram = gram_ref[...]
    wide = gram.astype(F32)
    norm_sq = jnp.sqrt(jnp.sum(wide * wide, keepdims=True)) + 1e-06
    inverse = 1.0 / norm_sq
    gradb = gradb_ref[...].reshape(blocks * 128, gradb_ref.shape[2])
    first = (gradb.astype(F32) * lax.rsqrt(norm_sq)).astype(BF16)

    def apply(value):
        return jnp.dot(gram, value, preferred_element_type=F32) * inverse

    second = (1.5 * first.astype(F32) - 0.5 * apply(first)).astype(BF16)
    power_one = apply(second)
    power_two = apply(power_one.astype(BF16))
    power_three = apply(power_two.astype(BF16))
    total = 1.5 * second.astype(F32) - 0.5 * (2.25 * power_one - 1.5 * power_two + 0.25 * power_three)
    out_ref[0] = total * width**0.5


def call(kernel, outs, ins, scratch=(), scalars=1, loose=0, vmem=24):
    return pl.pallas_call(
        kernel,
        out_shape=outs,
        in_specs=[smem_spec()] * scalars + [full_spec()] * (len(ins) - scalars - loose)
        + [pl.BlockSpec(memory_space=pl.ANY)] * loose,
        out_specs=jax.tree.map(lambda _: full_spec(), outs),
        scratch_shapes=list(scratch),
        compiler_params=pltpu.CompilerParams(vmem_limit_bytes=vmem * MIB),
    )(*ins)


def per_device(grad_out, hidden, gate_prob, expert_ids, weights):
    tokens, width_part = grad_out.shape
    top_count = expert_ids.shape[1]
    unit_part = hidden.shape[2]
    units = weights.shape[1]
    experts = lax.axis_size("x") * lax.axis_size("z")
    y_size = lax.axis_size("y")
    dp = y_size * 2
    width = width_part * dp
    capacity = 5 * tokens * top_count // (4 * experts)
    total_slots = experts * capacity
    pair_count = tokens * top_count
    y = lax.axis_index("y")
    c = lax.axis_index("c")
    block = jnp.arange(dp, dtype=jnp.int32)
    other_core = (block % 2) ^ c
    stands_at = other_core * y_size + block // 2
    goes_to = other_core * y_size + (block // 2 - y) % y_size
    came_from = other_core * y_size + (y - block // 2) % y_size
    spots = jnp.concatenate([stands_at, goes_to, came_from, jnp.full((1,), c)]).astype(jnp.int32)

    flat_ids = expert_ids.T.reshape(1, pair_count)
    named = (jnp.arange(experts, dtype=jnp.int32)[:, None] == flat_ids).astype(BF16)
    order = jnp.arange(pair_count, dtype=jnp.int32)
    earlier = (order[:, None] < order[None, :]).astype(BF16)
    before = jnp.dot(named, earlier, preferred_element_type=F32)
    rank_in = jnp.sum(before * named.astype(F32), axis=0, keepdims=True).astype(jnp.int32)
    late = rank_in >= 16
    main_index = jnp.where(late, -1, flat_ids * 16 + rank_in)
    column_blocks = width_part // 128
    tail = -(-4 * (column_blocks + 1) // 8) * 8
    left_index = jnp.where(late, flat_ids * tail + rank_in - 16, -1)

    scaled_part = (gate_prob[:, :, None] * hidden.astype(F32)).astype(BF16)
    scaled_part = scaled_part.transpose(1, 0, 2).reshape(pair_count, unit_part)

    def exchange(value, axes):
        return lax.all_to_all(value, axes, split_axis=0, concat_axis=0, tiled=True)

    sent = call(
        send_kernel,
        jax.ShapeDtypeStruct((experts, 16 * (column_blocks + 1) + tail, 128), BF16),
        (main_index, left_index, scaled_part, grad_out),
        scalars=0,
    )
    got = exchange(sent, EXPERT)

    dp_parts = jax.ShapeDtypeStruct((y_size, total_slots, unit_part), BF16)
    gathered = exchange(call(unpack_kernel, dp_parts, (got,), scalars=0, vmem=8), "y")
    gathered_other = swap_core(gathered)
    term_own, term_other, rows = call(
        back_kernel,
        (dp_parts, dp_parts, jax.ShapeDtypeStruct((total_slots, width_part), BF16)),
        (spots, got, weights[0]),
        vmem=20,
    )
    both = call(add_kernel, dp_parts, (term_own, swap_core(term_other), gathered), scalars=0, loose=1, vmem=8)
    summed = jnp.sum(exchange(both, "y").astype(F32), axis=0).astype(BF16)
    main_count = experts * 16
    returned = exchange(
        jnp.concatenate(
            [
                summed[:main_count].reshape(experts, 16, unit_part),
                summed[main_count:].reshape(experts, capacity - 16, unit_part),
            ],
            axis=1,
        ),
        EXPERT,
    ).reshape(total_slots, unit_part)
    slot_index = flat_ids * capacity + rank_in
    chosen = (jnp.arange(total_slots, dtype=jnp.int32)[:, None] == slot_index).astype(BF16)
    picked = lax.dot_general(chosen, returned, (((0,), (0,)), ((), ())), preferred_element_type=F32)
    picked = picked.reshape(top_count, tokens, unit_part).transpose(1, 0, 2)
    hidden_grad = (gate_prob[:, :, None] * picked).astype(BF16)

    wide = pltpu.VMEM((total_slots, units // 2), BF16)
    own_half = call(
        grad_half_kernel,
        jax.ShapeDtypeStruct((y_size, 128, width_part), BF16),
        (gathered, rows),
        (wide,),
        scalars=0,
        vmem=10,
    )
    packs = jax.ShapeDtypeStruct((y_size, units // 2 + 64, 128), BF16)
    grad_bf16, pack_own, pack_other = call(
        grad_kernel,
        (jax.ShapeDtypeStruct((dp, 128, width_part), BF16), packs, packs),
        (spots, own_half, gathered_other, rows),
        (wide,),
        vmem=20,
    )

    def reduce_dp(own, other):
        both = (own.astype(F32) + swap_core(other).astype(F32)).astype(BF16)
        parts = [both[0]] + [shift_y(both[k], k, y_size) for k in range(1, y_size)]
        total = parts[0].astype(F32)
        for part in parts[1:]:
            total = total + part.astype(F32)
        return total.astype(BF16)

    pack = reduce_dp(pack_own, pack_other)
    pack_all = jnp.stack([pack] + [shift_y(pack, k, y_size) for k in range(1, y_size)])
    pack_all_other = swap_core(pack_all)
    update = call(
        lambda *refs: ortho_kernel(width, *refs),
        jax.ShapeDtypeStruct((1, units, width_part), F32),
        (spots, pack_all, pack_all_other, grad_bf16),
        (pltpu.VMEM((units, units), BF16),),
    )
    return (hidden_grad, update)


def solution(mesh):
    dp, experts = mesh.devices.shape
    x_size = 4
    split = Mesh(
        mesh.devices.reshape(dp // 2, 2, x_size, experts // x_size), ("y", "c", "x", "z")
    )
    rows, cols = ("x", "z"), ("y", "c")
    in_specs = (P(rows, cols), P(rows, None, cols), P(rows, None), P(rows, None), P(rows, None, cols))
    out_specs = (P(rows, None, cols), P(rows, None, cols))
    return jax.shard_map(per_device, mesh=split, in_specs=in_specs, out_specs=out_specs, check_vma=False)
```

```python
import jax
import jax.numpy as jnp
from jax import lax
from jax.experimental import pallas as pl
from jax.experimental.pallas import tpu as pltpu
from jax.sharding import Mesh, PartitionSpec as P

EXPERT = ("x", "z")
MIB = 1024 * 1024
BF16 = jnp.bfloat16
F32 = jnp.float32
SMEM = pl.BlockSpec(memory_space=pltpu.SMEM)
LOOSE = pl.BlockSpec(memory_space=pl.ANY)


def shift_y(value, step, size):
    return lax.ppermute(value, "y", [(i, (i + step) % size) for i in range(size)])


def swap_core(value):
    return lax.ppermute(value, "c", [(0, 1), (1, 0)])


def exchange(value, axes):
    return lax.all_to_all(value, axes, split_axis=0, concat_axis=0, tiled=True)


def nt_dot(left, right):
    return lax.dot_general(left, right, (((1,), (1,)), ((), ())), preferred_element_type=F32)


def nn_dot(left, right):
    return jnp.dot(left, right, preferred_element_type=F32)


def one_hot(rows, index):
    return jnp.where(rows == index, 1.0, 0.0).astype(BF16)


def row_numbers(count):
    return lax.broadcasted_iota(jnp.int32, (count, 1), 0)


def lane_numbers(count):
    return lax.broadcasted_iota(jnp.int32, (1, count), 1)


def send_scaled_kernel(main_ref, left_ref, scaled_ref, out_ref):
    experts = out_ref.shape[0]
    scaled = scaled_ref[...]
    part = nn_dot(one_hot(row_numbers(experts * 16), main_ref[...]), scaled).astype(BF16)
    out_ref[:, 0:16, :] = part.reshape(experts, 16, 128)
    part = nn_dot(one_hot(row_numbers(experts * 8), left_ref[...]), scaled)
    out_ref[:, 16:24, :] = part.reshape(experts, 8, 128).astype(BF16)


def send_grad_kernel(main_ref, late_ref, grad_ref, out_ref):
    experts = out_ref.shape[0]
    tokens, width_part = grad_ref.shape
    blocks = width_part // 128
    grad = grad_ref[...]
    chosen = one_hot(row_numbers(experts * 16), main_ref[...])
    rows = nn_dot(chosen[:, :tokens] + chosen[:, tokens:], grad).astype(BF16)
    for b in range(blocks):
        out_ref[:, 16 * b : 16 * (b + 1), :] = rows[:, b * 128 : (b + 1) * 128].reshape(experts, 16, 128)
    number = row_numbers(experts * 16)
    chosen = one_hot((number & -16) + (number & 3), late_ref[...])
    rows = nn_dot(chosen[:, :tokens] + chosen[:, tokens:], grad)
    column = (number >> 2) & 3
    total = rows[:, 0:128]
    for b in range(1, blocks):
        total = jnp.where(column == b, rows[:, b * 128 : (b + 1) * 128], total)
    out_ref[:, 16 * blocks :, :] = total.astype(BF16).reshape(experts, 16, 128)


def unpack_kernel(got_ref, out_ref):
    experts = got_ref.shape[0]
    out_ref[: experts * 16] = got_ref[:, 0:16, :].reshape(experts * 16, 128)
    tail = got_ref[:, 16:24, :].astype(F32).reshape(experts * 8, 128).astype(BF16)
    number = row_numbers(experts * 4)
    take = one_hot((number >> 2) * 8 + (number & 3), lane_numbers(experts * 8))
    out_ref[experts * 16 :] = nn_dot(take, tail).astype(BF16)


def put_piece(spot, y_size, own_ref, other_ref, piece):
    @pl.when(spot < y_size)
    def _():
        own_ref[spot] = piece

    @pl.when(spot >= y_size)
    def _():
        other_ref[spot - y_size] = piece


def turn_kernel(spot_ref, own_ref, other_ref, out_ref):
    blocks = out_ref.shape[0] // 128
    y_size = blocks // 2
    for d in range(blocks):
        spot = spot_ref[blocks + d]

        @pl.when(spot < y_size)
        def _():
            out_ref[d * 128 : (d + 1) * 128, :] = own_ref[spot].T

        @pl.when(spot >= y_size)
        def _():
            out_ref[d * 128 : (d + 1) * 128, :] = other_ref[spot - y_size].T


def back_kernel(spot_ref, got_ref, weight_ref, after_ref, own_ref, other_ref, rows_ref):
    experts = got_ref.shape[0]
    columns = rows_ref.shape[1] // 128

    @pl.when(pl.program_id(0) == 0)
    def _():
        tail = got_ref[:, 16 * columns :, :].reshape(experts * 16, 128)
        number = row_numbers(experts * 4)
        base = (number >> 2) * 16 + (number & 3)
        for b in range(columns):
            lanes = slice(b * 128, (b + 1) * 128)
            rows_ref[: experts * 16, lanes] = got_ref[:, 16 * b : 16 * (b + 1), :].reshape(experts * 16, 128)
            take = one_hot(base + b * 4, lane_numbers(experts * 16))
            rows_ref[experts * 16 :, lanes] = nn_dot(take, tail).astype(BF16)

    term = nt_dot(rows_ref[...], weight_ref[...]).astype(BF16)
    core = spot_ref[spot_ref.shape[0] - 1]

    @pl.when(core == 0)
    def _():
        own_ref[0] = term[:, :128]
        other_ref[0] = term[:, 128:]

    @pl.when(core != 0)
    def _():
        own_ref[0] = term[:, 128:]
        other_ref[0] = term[:, :128]


def grad_kernel(spot_ref, turned_ref, rows_ref, gradb_ref, pack_own_ref, pack_other_ref):
    blocks = gradb_ref.shape[0] // 128
    y_size = blocks // 2
    half = blocks // 2
    step = pl.program_id(0)
    part = nn_dot(turned_ref[...], rows_ref[...]).astype(BF16)
    gradb_ref[pl.ds(pl.multiple_of(step * 256, 256), 256), :] = part

    @pl.when(step == pl.num_programs(0) - 1)
    def _():
        gradb = gradb_ref[...]
        gram = nt_dot(gradb, gradb).astype(BF16)
        for d in range(blocks):
            rows = slice(d * 128, (d + 1) * 128)
            pieces = []
            for k in range(half):
                j = (d + k) % blocks
                pieces.append(gram[rows, j * 128 : (j + 1) * 128])
            i = d % half
            top = i * 128 + (64 if d >= half else 0)
            pieces.append(gram[top : top + 64, (i + half) * 128 : (i + half + 1) * 128])
            spot = spot_ref[d]

            def put(ref, at):
                for k in range(half):
                    ref[at, k * 128 : (k + 1) * 128, :] = pieces[k]
                ref[at, half * 128 :, :] = pieces[half]

            @pl.when(spot < y_size)
            def _():
                put(pack_own_ref, spot)

            @pl.when(spot >= y_size)
            def _():
                put(pack_other_ref, spot - y_size)


def add_kernel(own_ref, other_ref, out_ref):
    out_ref[...] = (own_ref[...].astype(F32) + other_ref[...].astype(F32)).astype(BF16)


def pack_add_kernel(own_ref, other_ref, *out_refs):
    for k, out_ref in enumerate(out_refs):
        out_ref[...] = (own_ref[k].astype(F32) + other_ref[k].astype(F32)).astype(BF16)


def pack_sum_kernel(*refs):
    total = refs[0][...].astype(F32)
    for ref in refs[1:-1]:
        total = total + ref[...].astype(F32)
    refs[-1][...] = total.astype(BF16)


def return_kernel(part_ref, after_ref, out_ref):
    experts = out_ref.shape[0]
    total = part_ref[0].astype(F32)
    for k in range(1, part_ref.shape[0]):
        total = total + part_ref[k].astype(F32)
    total = total.astype(BF16)
    out_ref[:, 0:16, :] = total[: experts * 16].reshape(experts, 16, 128)
    number = row_numbers(experts * 8)
    wanted = jnp.where((number & 7) < 4, (number >> 3) * 4 + (number & 7), -1)
    left = nn_dot(one_hot(wanted, lane_numbers(experts * 4)), total[experts * 16 :])
    out_ref[:, 16:24, :] = left.reshape(experts, 8, 128).astype(BF16)


def ortho_kernel(width, spot_ref, own_ref, other_ref, gradb_ref, out_ref, gram_ref, norm_ref):
    blocks = gram_ref.shape[0] // 128
    y_size = blocks // 2
    half = blocks // 2

    @pl.when(pl.program_id(0) == 0)
    def _():
        unit = jnp.where(row_numbers(128) == lane_numbers(128), 1.0, 0.0).astype(BF16)
        for d in range(blocks):
            spot = spot_ref[blocks + d]

            def place(ref, at):
                for k in range(half):
                    j = (d + k) % blocks
                    gram_ref[d * 128 : (d + 1) * 128, j * 128 : (j + 1) * 128] = ref[at, k * 128 : (k + 1) * 128, :]
                turned = nt_dot(unit, ref[at, 128 : half * 128, :]).astype(BF16)
                for k in range(1, half):
                    j = (d + k) % blocks
                    gram_ref[j * 128 : (j + 1) * 128, d * 128 : (d + 1) * 128] = turned[:, (k - 1) * 128 : k * 128]
                i = d % half
                top = i * 128 + (64 if d >= half else 0)
                gram_ref[top : top + 64, (i + half) * 128 : (i + half + 1) * 128] = ref[at, half * 128 :, :]

            @pl.when(spot < y_size)
            def _():
                place(own_ref, spot)

            @pl.when(spot >= y_size)
            def _():
                place(other_ref, spot - y_size)

        for i in range(half):
            upper = gram_ref[i * 128 : (i + 1) * 128, (i + half) * 128 : (i + half + 1) * 128]
            gram_ref[(i + half) * 128 : (i + half + 1) * 128, i * 128 : (i + 1) * 128] = nt_dot(unit, upper).astype(BF16)
        squares = jnp.zeros((1, 1), F32)
        for ref in (own_ref, other_ref):
            whole = ref[...].astype(F32)
            diagonal = whole[:, :128, :]
            squares = squares + 2.0 * jnp.sum(whole * whole).reshape(1, 1) - jnp.sum(diagonal * diagonal).reshape(1, 1)
        norm_ref[...] = jnp.broadcast_to(jnp.sqrt(squares) + 1e-06, norm_ref.shape)

    norm_sq = norm_ref[0:1, 0:1]
    inverse = 1.0 / norm_sq
    gram = gram_ref[...]
    first = (gradb_ref[...].astype(F32) * lax.rsqrt(norm_sq)).astype(BF16)

    def apply(value):
        return nn_dot(gram, value) * inverse

    second = (1.5 * first.astype(F32) - 0.5 * apply(first)).astype(BF16)
    power_one = apply(second)
    power_two = apply(power_one.astype(BF16))
    power_three = apply(power_two.astype(BF16))
    total = 1.5 * second.astype(F32) - 0.5 * (2.25 * power_one - 1.5 * power_two + 0.25 * power_three)
    out_ref[0] = total * width**0.5


def whole(value):
    return pl.BlockSpec(value.shape, lambda *_: (0,) * len(value.shape))


def call(kernel, outs, ins, scratch=(), vmem=24, steps=(), specs=None, out_specs=None):
    specs = specs or {}
    out_specs = out_specs or {}
    flat, tree = jax.tree.flatten(outs)
    return pl.pallas_call(
        kernel,
        out_shape=outs,
        grid=steps,
        in_specs=[specs.get(i, whole(value)) for i, value in enumerate(ins)],
        out_specs=jax.tree.unflatten(tree, [out_specs.get(i, whole(value)) for i, value in enumerate(flat)]),
        scratch_shapes=list(scratch),
        compiler_params=pltpu.CompilerParams(vmem_limit_bytes=vmem * MIB),
    )(*ins)


def per_device(grad_out, hidden, gate_prob, expert_ids, weights):
    tokens, width_part = grad_out.shape
    top_count = expert_ids.shape[1]
    unit_part = hidden.shape[2]
    units = weights.shape[1]
    experts = lax.axis_size("x") * lax.axis_size("z")
    y_size = lax.axis_size("y")
    dp = y_size * 2
    width = width_part * dp
    capacity = 5 * tokens * top_count // (4 * experts)
    total_slots = experts * capacity
    pair_count = tokens * top_count
    y = lax.axis_index("y")
    c = lax.axis_index("c")
    block = jnp.arange(dp, dtype=jnp.int32)
    other_core = (block % 2) ^ c
    goes_to = other_core * y_size + (block // 2 - y) % y_size
    came_from = other_core * y_size + (y - block // 2) % y_size
    spots = jnp.concatenate([goes_to, came_from, jnp.full((1,), c)]).astype(jnp.int32)

    flat_ids = expert_ids.T.reshape(1, pair_count)
    named = (jnp.arange(experts, dtype=jnp.int32)[:, None] == flat_ids).astype(BF16)
    order = jnp.arange(pair_count, dtype=jnp.int32)
    earlier = (order[:, None] < order[None, :]).astype(BF16)
    before = jnp.dot(named, earlier, preferred_element_type=F32)
    rank_in = jnp.sum(before * named.astype(F32), axis=0, keepdims=True).astype(jnp.int32)
    late = rank_in >= 16
    main_index = jnp.where(late, -1, flat_ids * 16 + rank_in)
    left_index = jnp.where(late, flat_ids * 8 + rank_in - 16, -1)
    late_index = jnp.where(late, flat_ids * 16 + rank_in - 16, -1)

    scaled_part = (gate_prob[:, :, None] * hidden.astype(F32)).astype(BF16)
    scaled_part = scaled_part.transpose(1, 0, 2).reshape(pair_count, unit_part)
    columns = width_part // 128

    def shape(*dims):
        return jax.ShapeDtypeStruct(dims, BF16)

    got_scaled = exchange(
        call(send_scaled_kernel, shape(experts, 24, 128), (main_index, left_index, scaled_part)), EXPERT
    )
    got = exchange(
        call(send_grad_kernel, shape(experts, 20 * columns, 128), (main_index, late_index, grad_out)), EXPERT
    )

    scaled = call(unpack_kernel, shape(total_slots, unit_part), (got_scaled,), vmem=8)
    gathered = jnp.stack([scaled] + [shift_y(scaled, k, y_size) for k in range(1, y_size)])
    turned = call(
        turn_kernel, shape(units, total_slots), (spots, gathered, swap_core(gathered)), specs={0: SMEM}, vmem=20
    )

    piece = pl.BlockSpec((1, total_slots, 128), lambda i: (i, 0, 0))
    term_own, term_other, rows = call(
        back_kernel,
        (shape(y_size, total_slots, unit_part), shape(y_size, total_slots, unit_part), shape(total_slots, width_part)),
        (spots, got, pltpu.with_memory_space_constraint(weights[0], pltpu.HBM), turned),
        steps=(y_size,),
        specs={0: SMEM, 2: pl.BlockSpec((256, width_part), lambda i: (i, 0)), 3: LOOSE},
        out_specs={0: piece, 1: piece},
        vmem=20,
    )
    packs = shape(y_size, units // 2 + 64, 128)
    grad_bf16, pack_own, pack_other = call(
        grad_kernel,
        (shape(units, width_part), packs, packs),
        (spots, turned, rows),
        steps=(units // 256,),
        specs={0: SMEM, 1: pl.BlockSpec((256, total_slots), lambda i: (i, 0))},
        vmem=24,
    )
    both = call(
        add_kernel,
        shape(y_size, total_slots, unit_part),
        (term_own, swap_core(term_other)),
        steps=(y_size,),
        specs={0: piece, 1: piece},
        out_specs={0: piece},
        vmem=8,
    )
    parts = exchange(both, "y")

    pack = shape(units // 2 + 64, 128)
    pack_parts = call(pack_add_kernel, (pack,) * y_size, (pack_own, swap_core(pack_other)), vmem=8)
    pack_parts = [pack_parts[0]] + [shift_y(pack_parts[k], k, y_size) for k in range(1, y_size)]
    pack_total = call(pack_sum_kernel, pack, tuple(pack_parts), vmem=8)
    pack_all = jnp.stack([pack_total] + [shift_y(pack_total, k, y_size) for k in range(1, y_size)])
    pack_all_other = swap_core(pack_all)

    returned = exchange(
        call(return_kernel, shape(experts, 24, 128), (parts, pack_total), specs={1: LOOSE}, vmem=12), EXPERT
    ).reshape(experts * 24, unit_part)
    slot_index = flat_ids * 24 + rank_in
    chosen = (jnp.arange(experts * 24, dtype=jnp.int32)[:, None] == slot_index).astype(BF16)
    picked = lax.dot_general(chosen, returned, (((0,), (0,)), ((), ())), preferred_element_type=F32)
    picked = picked.reshape(top_count, tokens, unit_part).transpose(1, 0, 2)
    hidden_grad = (gate_prob[:, :, None] * picked).astype(BF16)

    half_width = width_part // 2
    update = call(
        lambda *refs: ortho_kernel(width, *refs),
        jax.ShapeDtypeStruct((1, units, width_part), F32),
        (spots, pack_all, pack_all_other, grad_bf16),
        (pltpu.VMEM((units, units), BF16), pltpu.VMEM((8, 128), F32)),
        steps=(2,),
        specs={0: SMEM, 3: pl.BlockSpec((units, half_width), lambda i: (0, i))},
        out_specs={0: pl.BlockSpec((1, units, half_width), lambda i: (0, 0, i))},
    )
    return (hidden_grad, update)


def solution(mesh):
    dp, experts = mesh.devices.shape
    x_size = 4
    split = Mesh(
        mesh.devices.reshape(dp // 2, 2, x_size, experts // x_size), ("y", "c", "x", "z")
    )
    rows, cols = ("x", "z"), ("y", "c")
    in_specs = (P(rows, cols), P(rows, None, cols), P(rows, None), P(rows, None), P(rows, None, cols))
    out_specs = (P(rows, None, cols), P(rows, None, cols))
    return jax.shard_map(per_device, mesh=split, in_specs=in_specs, out_specs=out_specs, check_vma=False)
```

```python
import jax
import jax.numpy as jnp
from jax import lax
from jax.experimental import pallas as pl
from jax.experimental.pallas import tpu as pltpu
from jax.sharding import Mesh, PartitionSpec as P

EXPERT = ("x", "z")
MIB = 1024 * 1024
BF16 = jnp.bfloat16
F32 = jnp.float32
SMEM = pl.BlockSpec(memory_space=pltpu.SMEM)
LOOSE = pl.BlockSpec(memory_space=pl.ANY)
HBM = pl.BlockSpec(memory_space=pltpu.HBM)


def shift_y(value, step, size):
    return lax.ppermute(value, "y", [(i, (i + step) % size) for i in range(size)])


def swap_y(value, flip, size):
    return lax.ppermute(value, "y", [(i, i ^ flip) for i in range(size)])


def swap_core(value):
    return lax.ppermute(value, "c", [(0, 1), (1, 0)])


def exchange(value, axes):
    return lax.all_to_all(value, axes, split_axis=0, concat_axis=0, tiled=True)


def nt_dot(left, right):
    return lax.dot_general(left, right, (((1,), (1,)), ((), ())), preferred_element_type=F32)


def nn_dot(left, right):
    return jnp.dot(left, right, preferred_element_type=F32)


def one_hot(rows, index):
    return jnp.where(rows == index, 1.0, 0.0).astype(BF16)


def row_numbers(count):
    return lax.broadcasted_iota(jnp.int32, (count, 1), 0)


def lane_numbers(count):
    return lax.broadcasted_iota(jnp.int32, (1, count), 1)


def send_scaled_kernel(main_ref, left_ref, scaled_ref, out_ref):
    experts = out_ref.shape[0]
    scaled = scaled_ref[...]
    part = nn_dot(one_hot(row_numbers(experts * 16), main_ref[...]), scaled).astype(BF16)
    out_ref[:, 0:16, :] = part.reshape(experts, 16, 128)
    part = nn_dot(one_hot(row_numbers(experts * 8), left_ref[...]), scaled)
    out_ref[:, 16:24, :] = part.reshape(experts, 8, 128).astype(BF16)


def send_grad_kernel(main_ref, late_ref, grad_ref, out_ref):
    experts = out_ref.shape[0]
    tokens, width_part = grad_ref.shape
    blocks = width_part // 128
    grad = grad_ref[...]
    chosen = one_hot(row_numbers(experts * 16), main_ref[...])
    rows = nn_dot(chosen[:, :tokens] + chosen[:, tokens:], grad).astype(BF16)
    for b in range(blocks):
        out_ref[:, 16 * b : 16 * (b + 1), :] = rows[:, b * 128 : (b + 1) * 128].reshape(experts, 16, 128)
    number = row_numbers(experts * 16)
    chosen = one_hot((number & -16) + (number & 3), late_ref[...])
    rows = nn_dot(chosen[:, :tokens] + chosen[:, tokens:], grad)
    column = (number >> 2) & 3
    total = rows[:, 0:128]
    for b in range(1, blocks):
        total = jnp.where(column == b, rows[:, b * 128 : (b + 1) * 128], total)
    out_ref[:, 16 * blocks :, :] = total.astype(BF16).reshape(experts, 16, 128)


def unpack_kernel(got_ref, out_ref):
    experts = got_ref.shape[0]
    out_ref[: experts * 16] = got_ref[:, 0:16, :].reshape(experts * 16, 128)
    tail = got_ref[:, 16:24, :].astype(F32).reshape(experts * 8, 128).astype(BF16)
    number = row_numbers(experts * 4)
    take = one_hot((number >> 2) * 8 + (number & 3), lane_numbers(experts * 8))
    out_ref[experts * 16 :] = nn_dot(take, tail).astype(BF16)


def turn_kernel(spot_ref, own_ref, other_ref, out_ref):
    blocks = out_ref.shape[0] // 128
    y_size = blocks // 2
    for d in range(blocks):
        spot = spot_ref[d]

        @pl.when(spot < y_size)
        def _():
            out_ref[d * 128 : (d + 1) * 128, :] = own_ref[spot].T

        @pl.when(spot >= y_size)
        def _():
            out_ref[d * 128 : (d + 1) * 128, :] = other_ref[spot - y_size].T


def core_kernel(
    spot_ref, got_hbm, weight_hbm, turned_hbm, after_ref,
    own_ref, other_ref, gradb_hbm, pack_own_ref, pack_other_ref,
    rows_ref, got_ref, weight_ref, turned_ref, gradb_ref, sems,
):
    fetch_got = pltpu.make_async_copy(got_hbm, got_ref, sems.at[0])
    fetch_weight = pltpu.make_async_copy(weight_hbm, weight_ref, sems.at[1])
    fetch_turned = pltpu.make_async_copy(turned_hbm, turned_ref, sems.at[2])
    fetch_got.start()
    fetch_weight.start()
    fetch_turned.start()
    experts = got_ref.shape[0]
    columns = rows_ref.shape[1] // 128
    blocks = weight_ref.shape[0] // 128
    y_size = blocks // 2
    half = blocks // 2
    number = row_numbers(256)
    order = one_hot(((number >> 2) & 15) * 16 + (number >> 6) * 4 + (number & 3), lane_numbers(256))
    fetch_got.wait()
    for b in range(columns):
        rows_ref[: experts * 16, b * 128 : (b + 1) * 128] = got_ref[:, 16 * b : 16 * (b + 1), :].reshape(
            experts * 16, 128
        )
    for s in range(experts // 16):
        late = nn_dot(order, got_ref[16 * s : 16 * (s + 1), 16 * columns :, :].reshape(256, 128)).astype(BF16)
        for b in range(columns):
            rows_ref[experts * 16 + s * 64 : experts * 16 + (s + 1) * 64, b * 128 : (b + 1) * 128] = late[
                b * 64 : (b + 1) * 64
            ]
    rows = rows_ref[...]

    fetch_weight.wait()
    term = nt_dot(rows, weight_ref[...]).astype(BF16)
    core = spot_ref[blocks]

    def put_terms(own, other):
        for k in range(y_size):
            own_ref[k] = term[:, (2 * k + own) * 128 : (2 * k + own + 1) * 128]
            other_ref[k] = term[:, (2 * k + other) * 128 : (2 * k + other + 1) * 128]

    @pl.when(core == 0)
    def _():
        put_terms(0, 1)

    @pl.when(core != 0)
    def _():
        put_terms(1, 0)

    fetch_turned.wait()
    gradb = nn_dot(turned_ref[...], rows).astype(BF16)
    gradb_ref[...] = gradb
    store_grad = pltpu.make_async_copy(gradb_ref, gradb_hbm, sems.at[3])
    store_grad.start()
    gram = nt_dot(gradb, gradb).astype(BF16)
    for d in range(blocks):
        i = d % half
        top = i * 128 + (64 if d >= half else 0)
        spot = spot_ref[d]

        def put(ref, at):
            for k in range(half):
                j = (d + k) % blocks
                ref[at, k * 128 : (k + 1) * 128, :] = gram[d * 128 : (d + 1) * 128, j * 128 : (j + 1) * 128]
            ref[at, half * 128 :, :] = gram[top : top + 64, (i + half) * 128 : (i + half + 1) * 128]

        @pl.when(spot < y_size)
        def _():
            put(pack_own_ref, spot)

        @pl.when(spot >= y_size)
        def _():
            put(pack_other_ref, spot - y_size)

    store_grad.wait()


def add_kernel(own_ref, other_ref, out_ref):
    out_ref[...] = (own_ref[...].astype(F32) + other_ref[...].astype(F32)).astype(BF16)


def pack_add_kernel(own_ref, other_ref, keep_ref, send_ref):
    near = keep_ref.shape[0]
    keep_ref[...] = (own_ref[:near].astype(F32) + other_ref[:near].astype(F32)).astype(BF16)
    send_ref[...] = (own_ref[near:].astype(F32) + other_ref[near:].astype(F32)).astype(BF16)


def pack_pair_kernel(keep_ref, got_ref, mine_ref, send_ref):
    mine_ref[...] = (keep_ref[0].astype(F32) + got_ref[0].astype(F32)).astype(BF16)
    send_ref[...] = (keep_ref[1].astype(F32) + got_ref[1].astype(F32)).astype(BF16)


def return_kernel(part_ref, after_ref, out_ref):
    experts = out_ref.shape[0]
    total = part_ref[0].astype(F32)
    for k in range(1, part_ref.shape[0]):
        total = total + part_ref[k].astype(F32)
    total = total.astype(BF16)
    out_ref[:, 0:16, :] = total[: experts * 16].reshape(experts, 16, 128)
    number = row_numbers(128)
    take = one_hot(jnp.where((number & 7) < 4, (number >> 3) * 4 + (number & 7), -1), lane_numbers(64))
    for s in range(experts // 16):
        left = nn_dot(take, total[experts * 16 + s * 64 : experts * 16 + (s + 1) * 64])
        out_ref[16 * s : 16 * (s + 1), 16:24, :] = left.reshape(16, 8, 128).astype(BF16)


def ortho_kernel(
    width, spot_ref, own_near_ref, own_far_ref, other_near_ref, other_far_ref, gradb_hbm, out_ref,
    gram_ref, pack_ref, gradb_ref, sem,
):
    fetch_grad = pltpu.make_async_copy(gradb_hbm, gradb_ref, sem)
    fetch_grad.start()
    blocks = gram_ref.shape[0] // 128
    half = blocks // 2
    squares = jnp.zeros((8, 128), F32)
    for i, ref in enumerate((own_near_ref, own_far_ref, other_near_ref, other_far_ref)):
        for k in range(2):
            pack = ref[k]
            pack_ref[2 * i + k] = pack
            square = pack.astype(F32)
            square = square * square
            squares = squares + 2.0 * jnp.sum(square.reshape(-1, 8, 128), axis=0)
            squares = squares - jnp.sum(square[:128].reshape(-1, 8, 128), axis=0)
    norm_sq = jnp.sqrt(jnp.sum(squares, keepdims=True)) + 1e-06
    for d in range(blocks):
        spot = spot_ref[d]
        rows = slice(d * 128, (d + 1) * 128)
        for k in range(half):
            lanes = slice((d + k) % blocks * 128, ((d + k) % blocks + 1) * 128)
            block = pack_ref[spot, k * 128 : (k + 1) * 128, :]
            gram_ref[rows, lanes] = block
            if k > 0:
                gram_ref[lanes, rows] = block.T
        i = d % half
        top = i * 128 + (64 if d >= half else 0)
        gram_ref[top : top + 64, (i + half) * 128 : (i + half + 1) * 128] = pack_ref[spot, half * 128 :, :]
    for i in range(half):
        upper = gram_ref[i * 128 : (i + 1) * 128, (i + half) * 128 : (i + half + 1) * 128]
        gram_ref[(i + half) * 128 : (i + half + 1) * 128, i * 128 : (i + 1) * 128] = upper.T

    inverse = 1.0 / norm_sq
    gram = gram_ref[...]
    fetch_grad.wait()
    first = (gradb_ref[...].astype(F32) * lax.rsqrt(norm_sq)).astype(BF16)

    def apply(value):
        return nn_dot(gram, value) * inverse

    second = (1.5 * first.astype(F32) - 0.5 * apply(first)).astype(BF16)
    power_one = apply(second).astype(BF16)
    power_two = apply(power_one).astype(BF16)
    power_three = apply(power_two)
    total = 1.5 * second.astype(F32)
    total = total - 0.5 * (2.25 * power_one.astype(F32) - 1.5 * power_two.astype(F32) + 0.25 * power_three)
    out_ref[0] = total * width**0.5


def in_hbm(value):
    return pltpu.with_memory_space_constraint(value, pltpu.HBM)


def whole(value):
    return pl.BlockSpec(value.shape, lambda *_: (0,) * len(value.shape))


def call(kernel, outs, ins, scratch=(), vmem=24, steps=(), specs=None, out_specs=None):
    specs = specs or {}
    out_specs = out_specs or {}
    flat, tree = jax.tree.flatten(outs)
    return pl.pallas_call(
        kernel,
        out_shape=outs,
        grid=steps,
        in_specs=[specs.get(i, whole(value)) for i, value in enumerate(ins)],
        out_specs=jax.tree.unflatten(tree, [out_specs.get(i, whole(value)) for i, value in enumerate(flat)]),
        scratch_shapes=list(scratch),
        compiler_params=pltpu.CompilerParams(vmem_limit_bytes=vmem * MIB),
    )(*ins)


def per_device(grad_out, hidden, gate_prob, expert_ids, weights):
    tokens, width_part = grad_out.shape
    top_count = expert_ids.shape[1]
    unit_part = hidden.shape[2]
    units = weights.shape[1]
    experts = lax.axis_size("x") * lax.axis_size("z")
    y_size = lax.axis_size("y")
    dp = y_size * 2
    width = width_part * dp
    capacity = 5 * tokens * top_count // (4 * experts)
    total_slots = experts * capacity
    pair_count = tokens * top_count
    y = lax.axis_index("y")
    c = lax.axis_index("c")
    block = jnp.arange(dp, dtype=jnp.int32)
    other_core = (block % 2) ^ c
    flip = y ^ (block // 2)
    pair_spot = other_core * y_size + (flip ^ (flip >> 1))
    came_from = other_core * y_size + (y - block // 2) % y_size
    core = jnp.full((1,), c)
    pair_spots = jnp.concatenate([pair_spot, core]).astype(jnp.int32)

    flat_ids = expert_ids.T.reshape(1, pair_count)
    named = (jnp.arange(experts, dtype=jnp.int32)[:, None] == flat_ids).astype(BF16)
    order = jnp.arange(pair_count, dtype=jnp.int32)
    earlier = (order[:, None] < order[None, :]).astype(BF16)
    before = jnp.dot(named, earlier, preferred_element_type=F32)
    rank_in = jnp.sum(before * named.astype(F32), axis=0, keepdims=True).astype(jnp.int32)
    late = rank_in >= 16
    main_index = jnp.where(late, -1, flat_ids * 16 + rank_in)
    left_index = jnp.where(late, flat_ids * 8 + rank_in - 16, -1)
    late_index = jnp.where(late, flat_ids * 16 + rank_in - 16, -1)

    scaled_part = (gate_prob[:, :, None] * hidden.astype(F32)).astype(BF16)
    scaled_part = scaled_part.transpose(1, 0, 2).reshape(pair_count, unit_part)
    columns = width_part // 128

    def shape(*dims):
        return jax.ShapeDtypeStruct(dims, BF16)

    got_scaled = exchange(
        call(send_scaled_kernel, shape(experts, 24, 128), (main_index, left_index, scaled_part)), EXPERT
    )
    got = exchange(
        call(send_grad_kernel, shape(experts, 20 * columns, 128), (main_index, late_index, grad_out)), EXPERT
    )

    scaled = call(unpack_kernel, shape(total_slots, unit_part), (got_scaled,), vmem=8)
    gathered = jnp.stack([scaled] + [shift_y(scaled, k, y_size) for k in range(1, y_size)])
    turned = call(
        turn_kernel, pltpu.HBM((units, total_slots), BF16), (came_from.astype(jnp.int32), gathered, swap_core(gathered)),
        specs={0: SMEM},
        vmem=20,
    )

    slot_index = flat_ids.reshape(pair_count, 1) * 24 + rank_in.reshape(pair_count, 1)
    chosen = (slot_index == jnp.arange(experts * 24, dtype=jnp.int32)[None, :]).astype(BF16)
    chosen = lax.optimization_barrier(chosen)

    dp_parts = shape(y_size, total_slots, unit_part)
    packs = shape(y_size, units // 2 + 64, 128)
    term_own, term_other, grad_bf16, pack_own, pack_other = call(
        core_kernel,
        (dp_parts, dp_parts, pltpu.HBM((units, width_part), BF16), pltpu.HBM(packs.shape, BF16), packs),
        (pair_spots, in_hbm(got), in_hbm(weights[0]), in_hbm(turned), chosen),
        (
            pltpu.VMEM((total_slots, width_part), BF16),
            pltpu.VMEM(got.shape, BF16),
            pltpu.VMEM((units, width_part), BF16),
            pltpu.VMEM((units, total_slots), BF16),
            pltpu.VMEM((units, width_part), BF16),
            pltpu.SemaphoreType.DMA((4,)),
        ),
        specs={0: SMEM, 1: HBM, 2: HBM, 3: HBM, 4: LOOSE},
        out_specs={2: HBM},
        vmem=32,
    )
    pack_swapped = swap_core(pack_other)
    piece = pl.BlockSpec((1, total_slots, 128), lambda i: (i, 0, 0))
    both = call(
        add_kernel,
        pltpu.HBM(dp_parts.shape, BF16),
        (term_own, swap_core(term_other)),
        steps=(y_size,),
        specs={0: piece, 1: piece},
        out_specs={0: piece},
        vmem=8,
    )
    parts = exchange(both, "y")

    pack = shape(units // 2 + 64, 128)
    pair = shape(2, units // 2 + 64, 128)
    keep, send = call(pack_add_kernel, (pair, pair), (in_hbm(pack_own), pack_swapped), vmem=8)
    mine, send = call(pack_pair_kernel, (pack, pack), (keep, swap_y(send, 3, y_size)), vmem=8)
    mine = call(add_kernel, pack, (mine, swap_y(send, 1, y_size)), vmem=8)

    returned = exchange(
        call(return_kernel, shape(experts, 24, 128), (parts, mine), specs={1: LOOSE}, vmem=12), EXPERT
    ).reshape(experts * 24, unit_part)
    picked = jnp.dot(chosen, returned, preferred_element_type=F32)
    picked = picked.reshape(top_count, tokens, unit_part).transpose(1, 0, 2)
    hidden_grad = (gate_prob[:, :, None] * picked).astype(BF16)

    near = jnp.stack([mine, swap_y(mine, 1, y_size)])
    far = swap_y(near, 3, y_size)
    update = call(
        lambda *refs: ortho_kernel(width, *refs),
        jax.ShapeDtypeStruct((1, units, width_part), F32),
        (pair_spots, near, far, swap_core(near), swap_core(far), in_hbm(grad_bf16)),
        (
            pltpu.VMEM((units, units), BF16),
            pltpu.VMEM((dp, units // 2 + 64, 128), BF16),
            pltpu.VMEM((units, width_part), BF16),
            pltpu.SemaphoreType.DMA,
        ),
        specs={0: SMEM, 5: HBM},
        vmem=32,
    )
    return (hidden_grad, update)


def solution(mesh):
    dp, experts = mesh.devices.shape
    x_size = 4
    split = Mesh(
        mesh.devices.reshape(dp // 2, 2, x_size, experts // x_size), ("y", "c", "x", "z")
    )
    rows, cols = ("x", "z"), ("y", "c")
    in_specs = (P(rows, cols), P(rows, None, cols), P(rows, None), P(rows, None), P(rows, None, cols))
    out_specs = (P(rows, None, cols), P(rows, None, cols))
    return jax.shard_map(per_device, mesh=split, in_specs=in_specs, out_specs=out_specs, check_vma=False)
```

```python
import jax
import jax.numpy as jnp
from jax import lax
from jax.experimental import pallas as pl
from jax.experimental.pallas import tpu as pltpu
from jax.sharding import Mesh, PartitionSpec as P

EXPERT = ("x", "z")
MIB = 1024 * 1024
BF16 = jnp.bfloat16
F32 = jnp.float32
SMEM = pl.BlockSpec(memory_space=pltpu.SMEM)
LOOSE = pl.BlockSpec(memory_space=pl.ANY)
HBM = pl.BlockSpec(memory_space=pltpu.HBM)


def shift_y(value, step, size):
    return lax.ppermute(value, "y", [(i, (i + step) % size) for i in range(size)])


def swap_y(value, flip, size):
    return lax.ppermute(value, "y", [(i, i ^ flip) for i in range(size)])


def swap_core(value):
    return lax.ppermute(value, "c", [(0, 1), (1, 0)])


def exchange(value, axes):
    return lax.all_to_all(value, axes, split_axis=0, concat_axis=0, tiled=True)


def nt_dot(left, right):
    return lax.dot_general(left, right, (((1,), (1,)), ((), ())), preferred_element_type=F32)


def nn_dot(left, right):
    return jnp.dot(left, right, preferred_element_type=F32)


def one_hot(rows, index):
    return jnp.where(rows == index, 1.0, 0.0).astype(BF16)


def row_numbers(count):
    return lax.broadcasted_iota(jnp.int32, (count, 1), 0)


def lane_numbers(count):
    return lax.broadcasted_iota(jnp.int32, (1, count), 1)


def send_scaled_kernel(main_ref, left_ref, scaled_ref, out_ref):
    experts = out_ref.shape[0]
    scaled = scaled_ref[...]
    part = nn_dot(one_hot(row_numbers(experts * 16), main_ref[...]), scaled).astype(BF16)
    out_ref[:, 0:16, :] = part.reshape(experts, 16, 128)
    part = nn_dot(one_hot(row_numbers(experts * 8), left_ref[...]), scaled)
    out_ref[:, 16:24, :] = part.reshape(experts, 8, 128).astype(BF16)


def send_grad_kernel(main_ref, late_ref, grad_ref, out_ref):
    experts = out_ref.shape[0]
    tokens, width_part = grad_ref.shape
    blocks = width_part // 128
    grad = grad_ref[...]
    chosen = one_hot(row_numbers(experts * 16), main_ref[...])
    rows = nn_dot(chosen[:, :tokens] + chosen[:, tokens:], grad).astype(BF16)
    for b in range(blocks):
        out_ref[:, 16 * b : 16 * (b + 1), :] = rows[:, b * 128 : (b + 1) * 128].reshape(experts, 16, 128)
    number = row_numbers(experts * 16)
    chosen = one_hot((number & -16) + (number & 3), late_ref[...])
    rows = nn_dot(chosen[:, :tokens] + chosen[:, tokens:], grad)
    column = (number >> 2) & 3
    total = rows[:, 0:128]
    for b in range(1, blocks):
        total = jnp.where(column == b, rows[:, b * 128 : (b + 1) * 128], total)
    out_ref[:, 16 * blocks :, :] = total.astype(BF16).reshape(experts, 16, 128)


def unpack_kernel(got_ref, out_ref):
    experts = got_ref.shape[0]
    out_ref[: experts * 16] = got_ref[:, 0:16, :].reshape(experts * 16, 128)
    tail = got_ref[:, 16:24, :].astype(F32).reshape(experts * 8, 128).astype(BF16)
    number = row_numbers(experts * 4)
    take = one_hot((number >> 2) * 8 + (number & 3), lane_numbers(experts * 8))
    out_ref[experts * 16 :] = nn_dot(take, tail).astype(BF16)


def turn_kernel(spot_ref, own_ref, other_ref, out_ref):
    blocks = out_ref.shape[0] // 128
    y_size = blocks // 2
    for d in range(blocks):
        spot = spot_ref[d]

        @pl.when(spot < y_size)
        def _():
            out_ref[d * 128 : (d + 1) * 128, :] = own_ref[spot].T

        @pl.when(spot >= y_size)
        def _():
            out_ref[d * 128 : (d + 1) * 128, :] = other_ref[spot - y_size].T


def core_kernel(
    spot_ref, got_hbm, weight_hbm, turned_hbm,
    own_ref, other_ref, gradb_hbm, pack_own_ref, pack_other_ref,
    rows_ref, got_ref, weight_ref, turned_ref, gradb_ref, sems,
):
    experts = got_ref.shape[0]
    columns = rows_ref.shape[1] // 128
    blocks = weight_ref.shape[0] // 128
    y_size = blocks // 2
    half = blocks // 2
    groups = experts // 16
    part = weight_ref.shape[0] // groups

    def fetch(source, target, size, first):
        copies = []
        for s in range(groups):
            here = slice(s * size, (s + 1) * size)
            copies.append(pltpu.make_async_copy(source.at[here], target.at[here], sems.at[first + s]))
            copies[-1].start()
        return copies

    fetch_got = fetch(got_hbm, got_ref, 16, 0)
    fetch_weight = fetch(weight_hbm, weight_ref, part, groups)
    fetch_turned = fetch(turned_hbm, turned_ref, part, 2 * groups)

    number = row_numbers(256)
    order = one_hot(((number >> 2) & 15) * 16 + (number >> 6) * 4 + (number & 3), lane_numbers(256))
    for s in range(groups):
        fetch_got[s].wait()
        here = slice(16 * s, 16 * (s + 1))
        late = nn_dot(order, got_ref[here, 16 * columns :, :].reshape(256, 128)).astype(BF16)
        for b in range(columns):
            lanes = slice(b * 128, (b + 1) * 128)
            rows_ref[256 * s : 256 * (s + 1), lanes] = got_ref[here, 16 * b : 16 * (b + 1), :].reshape(256, 128)
            rows_ref[experts * 16 + s * 64 : experts * 16 + (s + 1) * 64, lanes] = late[b * 64 : (b + 1) * 64]
    rows = rows_ref[...]
    core = spot_ref[blocks]

    for copy in fetch_weight:
        copy.wait()
    term = nt_dot(rows, weight_ref[...]).astype(BF16)

    def put_terms(own, other):
        for k in range(y_size):
            own_ref[k] = term[:, (2 * k + own) * 128 : (2 * k + own + 1) * 128]
            other_ref[k] = term[:, (2 * k + other) * 128 : (2 * k + other + 1) * 128]

    @pl.when(core == 0)
    def _():
        put_terms(0, 1)

    @pl.when(core != 0)
    def _():
        put_terms(1, 0)

    for copy in fetch_turned:
        copy.wait()
    gradb = nn_dot(turned_ref[...], rows).astype(BF16)
    gradb_ref[...] = gradb
    store_grad = pltpu.make_async_copy(gradb_ref, gradb_hbm, sems.at[3 * groups])
    store_grad.start()
    gram = nt_dot(gradb, gradb).astype(BF16)

    def put_packs(ref, side):
        for n in range(y_size):
            d = 2 * n + side
            i = d % half
            top = i * 128 + (64 if d >= half else 0)
            for k in range(half):
                j = (d + k) % blocks
                ref[n, k * 128 : (k + 1) * 128, :] = gram[d * 128 : (d + 1) * 128, j * 128 : (j + 1) * 128]
            ref[n, half * 128 :, :] = gram[top : top + 64, (i + half) * 128 : (i + half + 1) * 128]

    @pl.when(core == 0)
    def _():
        put_packs(pack_own_ref, 0)
        put_packs(pack_other_ref, 1)

    @pl.when(core != 0)
    def _():
        put_packs(pack_own_ref, 1)
        put_packs(pack_other_ref, 0)

    store_grad.wait()


def add_kernel(own_ref, other_ref, pack_own_ref, pack_other_ref, out_ref):
    count = own_ref.shape[1]
    out_ref[:, :count] = (own_ref[...].astype(F32) + other_ref[...].astype(F32)).astype(BF16)
    out_ref[:, count:] = (pack_own_ref[...].astype(F32) + pack_other_ref[...].astype(F32)).astype(BF16)


def return_kernel(part_hbm, out_ref, pack_ref, part_ref, sems):
    experts = out_ref.shape[0]
    count = part_ref.shape[1] - pack_ref.shape[0]
    copies = []
    for k in range(part_ref.shape[0]):
        copies.append(pltpu.make_async_copy(part_hbm.at[k], part_ref.at[k], sems.at[k]))
        copies[-1].start()
    number = row_numbers(128)
    take = one_hot(jnp.where((number & 7) < 4, (number >> 3) * 4 + (number & 7), -1), lane_numbers(64))
    for copy in copies:
        copy.wait()
    total = part_ref[0].astype(F32)
    for k in range(1, part_ref.shape[0]):
        total = total + part_ref[k].astype(F32)
    total = total.astype(BF16)
    pack_ref[...] = total[count:]
    out_ref[:, 0:16, :] = total[: experts * 16].reshape(experts, 16, 128)
    for s in range(experts // 16):
        left = nn_dot(take, total[experts * 16 + s * 64 : experts * 16 + (s + 1) * 64])
        out_ref[16 * s : 16 * (s + 1), 16:24, :] = left.reshape(16, 8, 128).astype(BF16)


def ortho_kernel(
    width, spot_ref, own_near_ref, own_far_ref, other_near_ref, other_far_ref, gradb_hbm, out_ref,
    gram_ref, pack_ref, gradb_ref, sem,
):
    fetch_grad = pltpu.make_async_copy(gradb_hbm, gradb_ref, sem)
    fetch_grad.start()
    blocks = gram_ref.shape[0] // 128
    half = blocks // 2
    squares = jnp.zeros((8, 128), F32)
    for i, ref in enumerate((own_near_ref, own_far_ref, other_near_ref, other_far_ref)):
        for k in range(2):
            pack = ref[k]
            pack_ref[2 * i + k] = pack
            square = pack.astype(F32)
            square = square * square
            squares = squares + 2.0 * jnp.sum(square.reshape(-1, 8, 128), axis=0)
            squares = squares - jnp.sum(square[:128].reshape(-1, 8, 128), axis=0)
    norm_sq = jnp.sqrt(jnp.sum(squares, keepdims=True)) + 1e-06
    for d in range(blocks):
        spot = spot_ref[d]
        rows = slice(d * 128, (d + 1) * 128)
        for k in range(half):
            lanes = slice((d + k) % blocks * 128, ((d + k) % blocks + 1) * 128)
            block = pack_ref[spot, k * 128 : (k + 1) * 128, :]
            gram_ref[rows, lanes] = block
            if k > 0:
                gram_ref[lanes, rows] = block.T
        i = d % half
        top = i * 128 + (64 if d >= half else 0)
        gram_ref[top : top + 64, (i + half) * 128 : (i + half + 1) * 128] = pack_ref[spot, half * 128 :, :]
    for i in range(half):
        upper = gram_ref[i * 128 : (i + 1) * 128, (i + half) * 128 : (i + half + 1) * 128]
        gram_ref[(i + half) * 128 : (i + half + 1) * 128, i * 128 : (i + 1) * 128] = upper.T

    inverse = 1.0 / norm_sq
    gram = gram_ref[...]
    fetch_grad.wait()
    first = (gradb_ref[...].astype(F32) * lax.rsqrt(norm_sq)).astype(BF16)

    def apply(value):
        return nn_dot(gram, value) * inverse

    second = (1.5 * first.astype(F32) - 0.5 * apply(first)).astype(BF16)
    power_one = apply(second).astype(BF16)
    power_two = apply(power_one).astype(BF16)
    power_three = apply(power_two)
    total = 1.5 * second.astype(F32)
    total = total - 0.5 * (2.25 * power_one.astype(F32) - 1.5 * power_two.astype(F32) + 0.25 * power_three)
    out_ref[0] = total * width**0.5


def in_hbm(value):
    return pltpu.with_memory_space_constraint(value, pltpu.HBM)


def whole(value):
    return pl.BlockSpec(value.shape, lambda *_: (0,) * len(value.shape))


def call(kernel, outs, ins, scratch=(), vmem=24, steps=(), specs=None, out_specs=None):
    specs = specs or {}
    out_specs = out_specs or {}
    flat, tree = jax.tree.flatten(outs)
    return pl.pallas_call(
        kernel,
        out_shape=outs,
        grid=steps,
        in_specs=[specs.get(i, whole(value)) for i, value in enumerate(ins)],
        out_specs=jax.tree.unflatten(tree, [out_specs.get(i, whole(value)) for i, value in enumerate(flat)]),
        scratch_shapes=list(scratch),
        compiler_params=pltpu.CompilerParams(vmem_limit_bytes=vmem * MIB),
    )(*ins)


def per_device(grad_out, hidden, gate_prob, expert_ids, weights):
    tokens, width_part = grad_out.shape
    top_count = expert_ids.shape[1]
    unit_part = hidden.shape[2]
    units = weights.shape[1]
    experts = lax.axis_size("x") * lax.axis_size("z")
    y_size = lax.axis_size("y")
    dp = y_size * 2
    width = width_part * dp
    capacity = 5 * tokens * top_count // (4 * experts)
    total_slots = experts * capacity
    pair_count = tokens * top_count
    y = lax.axis_index("y")
    c = lax.axis_index("c")
    block = jnp.arange(dp, dtype=jnp.int32)
    other_core = (block % 2) ^ c
    flip = y ^ (block // 2)
    pair_spot = other_core * y_size + (flip ^ (flip >> 1))
    came_from = other_core * y_size + (y - block // 2) % y_size
    core = jnp.full((1,), c)
    pair_spots = jnp.concatenate([pair_spot, core]).astype(jnp.int32)

    flat_ids = expert_ids.T.reshape(1, pair_count)
    named = (jnp.arange(experts, dtype=jnp.int32)[:, None] == flat_ids).astype(BF16)
    order = jnp.arange(pair_count, dtype=jnp.int32)
    earlier = (order[:, None] < order[None, :]).astype(BF16)
    before = jnp.dot(named, earlier, preferred_element_type=F32)
    rank_in = jnp.sum(before * named.astype(F32), axis=0, keepdims=True).astype(jnp.int32)
    late = rank_in >= 16
    main_index = jnp.where(late, -1, flat_ids * 16 + rank_in)
    left_index = jnp.where(late, flat_ids * 8 + rank_in - 16, -1)
    late_index = jnp.where(late, flat_ids * 16 + rank_in - 16, -1)

    scaled_part = (gate_prob[:, :, None] * hidden.astype(F32)).astype(BF16)
    scaled_part = scaled_part.transpose(1, 0, 2).reshape(pair_count, unit_part)
    columns = width_part // 128

    def shape(*dims):
        return jax.ShapeDtypeStruct(dims, BF16)

    got_scaled = exchange(
        call(send_scaled_kernel, shape(experts, 24, 128), (main_index, left_index, scaled_part)), EXPERT
    )
    got = exchange(
        call(send_grad_kernel, shape(experts, 20 * columns, 128), (main_index, late_index, grad_out)), EXPERT
    )

    scaled = call(unpack_kernel, shape(total_slots, unit_part), (got_scaled,), vmem=8)
    gathered = jnp.stack([scaled] + [shift_y(scaled, k, y_size) for k in range(1, y_size)])
    turned = call(
        turn_kernel, pltpu.HBM((units, total_slots), BF16), (came_from.astype(jnp.int32), gathered, swap_core(gathered)),
        specs={0: SMEM},
        vmem=20,
    )

    dp_parts = shape(y_size, total_slots, unit_part)
    pack_rows = units // 2 + 64
    packs = shape(y_size, pack_rows, 128)
    groups = experts // 16
    term_own, term_other, grad_bf16, pack_own, pack_other = call(
        core_kernel,
        (dp_parts, dp_parts, pltpu.HBM((units, width_part), BF16), packs, packs),
        (pair_spots, in_hbm(got), in_hbm(weights[0]), in_hbm(turned)),
        (
            pltpu.VMEM((total_slots, width_part), BF16),
            pltpu.VMEM(got.shape, BF16),
            pltpu.VMEM((units, width_part), BF16),
            pltpu.VMEM((units, total_slots), BF16),
            pltpu.VMEM((units, width_part), BF16),
            pltpu.SemaphoreType.DMA((3 * groups + 1,)),
        ),
        specs={0: SMEM, 1: HBM, 2: HBM, 3: HBM},
        out_specs={2: HBM},
        vmem=32,
    )

    def piece(count):
        return pl.BlockSpec((1, count, 128), lambda i: (i, 0, 0))

    both = call(
        add_kernel,
        pltpu.HBM((y_size, total_slots + pack_rows, 128), BF16),
        (term_own, swap_core(term_other), pack_own, swap_core(pack_other)),
        steps=(y_size,),
        specs={0: piece(total_slots), 1: piece(total_slots), 2: piece(pack_rows), 3: piece(pack_rows)},
        out_specs={0: piece(total_slots + pack_rows)},
        vmem=12,
    )
    parts = exchange(both, "y")
    sent_back, mine = call(
        return_kernel,
        (pltpu.HBM((experts, 24, 128), BF16), shape(pack_rows, 128)),
        (in_hbm(parts),),
        (pltpu.VMEM(parts.shape, BF16), pltpu.SemaphoreType.DMA((y_size,))),
        specs={0: HBM},
        vmem=16,
    )
    returned = exchange(sent_back, EXPERT).reshape(experts * 24, unit_part)
    slot_index = flat_ids * 24 + rank_in
    chosen = (jnp.arange(experts * 24, dtype=jnp.int32)[:, None] == slot_index).astype(BF16)
    picked = lax.dot_general(chosen, returned, (((0,), (0,)), ((), ())), preferred_element_type=F32)
    picked = picked.reshape(top_count, tokens, unit_part).transpose(1, 0, 2)
    hidden_grad = (gate_prob[:, :, None] * picked).astype(BF16)

    near = jnp.stack([mine, swap_y(mine, 1, y_size)])
    far = swap_y(near, 3, y_size)
    update = call(
        lambda *refs: ortho_kernel(width, *refs),
        jax.ShapeDtypeStruct((1, units, width_part), F32),
        (pair_spots, near, far, swap_core(near), swap_core(far), in_hbm(grad_bf16)),
        (
            pltpu.VMEM((units, units), BF16),
            pltpu.VMEM((dp, units // 2 + 64, 128), BF16),
            pltpu.VMEM((units, width_part), BF16),
            pltpu.SemaphoreType.DMA,
        ),
        specs={0: SMEM, 5: HBM},
        vmem=32,
    )
    return (hidden_grad, update)


def solution(mesh):
    dp, experts = mesh.devices.shape
    x_size = 4
    split = Mesh(
        mesh.devices.reshape(dp // 2, 2, x_size, experts // x_size), ("y", "c", "x", "z")
    )
    rows, cols = ("x", "z"), ("y", "c")
    in_specs = (P(rows, cols), P(rows, None, cols), P(rows, None), P(rows, None), P(rows, None, cols))
    out_specs = (P(rows, None, cols), P(rows, None, cols))
    return jax.shard_map(per_device, mesh=split, in_specs=in_specs, out_specs=out_specs, check_vma=False)
```

```python
import jax
import jax.numpy as jnp
from jax import lax
from jax.experimental import pallas as pl
from jax.experimental.pallas import tpu as pltpu
from jax.sharding import Mesh, PartitionSpec as P

EXPERT = ("x", "z")
MIB = 1024 * 1024
BF16 = jnp.bfloat16
F32 = jnp.float32
SMEM = pl.BlockSpec(memory_space=pltpu.SMEM)
LOOSE = pl.BlockSpec(memory_space=pl.ANY)
HBM = pl.BlockSpec(memory_space=pltpu.HBM)


def shift_y(value, step, size):
    return lax.ppermute(value, "y", [(i, (i + step) % size) for i in range(size)])


def swap_y(value, flip, size):
    return lax.ppermute(value, "y", [(i, i ^ flip) for i in range(size)])


def swap_core(value):
    return lax.ppermute(value, "c", [(0, 1), (1, 0)])


def exchange(value, axes):
    return lax.all_to_all(value, axes, split_axis=0, concat_axis=0, tiled=True)


def nt_dot(left, right):
    return lax.dot_general(left, right, (((1,), (1,)), ((), ())), preferred_element_type=F32)


def nn_dot(left, right):
    return jnp.dot(left, right, preferred_element_type=F32)


def one_hot(rows, index):
    return jnp.where(rows == index, 1.0, 0.0).astype(BF16)


def row_numbers(count):
    return lax.broadcasted_iota(jnp.int32, (count, 1), 0)


def lane_numbers(count):
    return lax.broadcasted_iota(jnp.int32, (1, count), 1)


def send_scaled_kernel(ids_ref, scaled_ref, out_ref, main_ref, late_ref, slot_ref):
    experts = out_ref.shape[0]
    count, tokens = ids_ref.shape
    earlier = jnp.where(row_numbers(tokens) < lane_numbers(tokens), 1.0, 0.0).astype(BF16)
    passed = jnp.zeros((experts, 1), F32)
    ids, ranks = [], []
    for k in range(count):
        ids.append(ids_ref[k : k + 1, :])
        named = one_hot(row_numbers(experts), ids[k])
        wide = named.astype(F32)
        before = nn_dot(named, earlier) + passed
        ranks.append(jnp.sum(wide * before, axis=0, keepdims=True).astype(jnp.int32))
        passed = passed + jnp.sum(wide, axis=1, keepdims=True)
    expert = jnp.concatenate(ids, axis=1)
    rank = jnp.concatenate(ranks, axis=1)
    late = rank >= 16
    main_index = jnp.where(late, -1, expert * 16 + rank)
    main_ref[...] = main_index
    late_ref[...] = jnp.where(late, expert * 16 + rank - 16, -1)
    slot_ref[...] = expert * 24 + rank
    left_index = jnp.where(late, expert * 8 + rank - 16, -1)
    scaled = scaled_ref[...]
    part = nn_dot(one_hot(row_numbers(experts * 16), main_index), scaled).astype(BF16)
    out_ref[:, 0:16, :] = part.reshape(experts, 16, 128)
    part = nn_dot(one_hot(row_numbers(experts * 8), left_index), scaled)
    out_ref[:, 16:24, :] = part.reshape(experts, 8, 128).astype(BF16)


def send_grad_kernel(main_ref, late_ref, grad_ref, out_ref):
    experts = out_ref.shape[0]
    tokens, width_part = grad_ref.shape
    blocks = width_part // 128
    grad = grad_ref[...]
    chosen = one_hot(row_numbers(experts * 16), main_ref[...])
    rows = nn_dot(chosen[:, :tokens] + chosen[:, tokens:], grad).astype(BF16)
    for b in range(blocks):
        out_ref[:, 16 * b : 16 * (b + 1), :] = rows[:, b * 128 : (b + 1) * 128].reshape(experts, 16, 128)
    number = row_numbers(experts * 16)
    chosen = one_hot((number & -16) + (number & 3), late_ref[...])
    rows = nn_dot(chosen[:, :tokens] + chosen[:, tokens:], grad)
    column = (number >> 2) & 3
    total = rows[:, 0:128]
    for b in range(1, blocks):
        total = jnp.where(column == b, rows[:, b * 128 : (b + 1) * 128], total)
    out_ref[:, 16 * blocks :, :] = total.astype(BF16).reshape(experts, 16, 128)


def unpack_kernel(got_ref, out_ref):
    experts = got_ref.shape[0]
    out_ref[: experts * 16] = got_ref[:, 0:16, :].reshape(experts * 16, 128)
    tail = got_ref[:, 16:24, :].astype(F32).reshape(experts * 8, 128).astype(BF16)
    number = row_numbers(experts * 4)
    take = one_hot((number >> 2) * 8 + (number & 3), lane_numbers(experts * 8))
    out_ref[experts * 16 :] = nn_dot(take, tail).astype(BF16)


def turn_kernel(spot_ref, own_ref, other_ref, out_ref):
    blocks = out_ref.shape[0] // 128
    y_size = blocks // 2
    for d in range(blocks):
        spot = spot_ref[d]

        @pl.when(spot < y_size)
        def _():
            out_ref[d * 128 : (d + 1) * 128, :] = own_ref[spot].T

        @pl.when(spot >= y_size)
        def _():
            out_ref[d * 128 : (d + 1) * 128, :] = other_ref[spot - y_size].T


def core_kernel(
    spot_ref, got_hbm, weight_hbm, turned_hbm,
    own_ref, other_ref, gradb_hbm,
    rows_ref, got_ref, weight_ref, turned_ref, gradb_ref, sems,
):
    experts = got_ref.shape[0]
    columns = rows_ref.shape[1] // 128
    blocks = weight_ref.shape[0] // 128
    y_size = blocks // 2
    half = blocks // 2
    groups = experts // 16
    part = weight_ref.shape[0] // groups

    def fetch(source, target, size, first):
        copies = []
        for s in range(groups):
            here = slice(s * size, (s + 1) * size)
            copies.append(pltpu.make_async_copy(source.at[here], target.at[here], sems.at[first + s]))
            copies[-1].start()
        return copies

    fetch_got = fetch(got_hbm, got_ref, 16, 0)
    fetch_weight = fetch(weight_hbm, weight_ref, part, groups)
    fetch_turned = fetch(turned_hbm, turned_ref, part, 2 * groups)

    number = row_numbers(256)
    order = one_hot(((number >> 2) & 15) * 16 + (number >> 6) * 4 + (number & 3), lane_numbers(256))
    for s in range(groups):
        fetch_got[s].wait()
        here = slice(16 * s, 16 * (s + 1))
        late = nn_dot(order, got_ref[here, 16 * columns :, :].reshape(256, 128)).astype(BF16)
        for b in range(columns):
            lanes = slice(b * 128, (b + 1) * 128)
            rows_ref[256 * s : 256 * (s + 1), lanes] = got_ref[here, 16 * b : 16 * (b + 1), :].reshape(256, 128)
            rows_ref[experts * 16 + s * 64 : experts * 16 + (s + 1) * 64, lanes] = late[b * 64 : (b + 1) * 64]
    rows = rows_ref[...]
    core = spot_ref[blocks]
    count = rows_ref.shape[0]

    for copy in fetch_weight:
        copy.wait()
    term = nt_dot(rows, weight_ref[...]).astype(BF16)

    def put_terms(own, other):
        for k in range(y_size):
            own_ref[k, :count] = term[:, (2 * k + own) * 128 : (2 * k + own + 1) * 128]
            other_ref[k, :count] = term[:, (2 * k + other) * 128 : (2 * k + other + 1) * 128]

    @pl.when(core == 0)
    def _():
        put_terms(0, 1)

    @pl.when(core != 0)
    def _():
        put_terms(1, 0)

    for copy in fetch_turned:
        copy.wait()
    gradb = nn_dot(turned_ref[...], rows).astype(BF16)
    gradb_ref[...] = gradb
    store_grad = pltpu.make_async_copy(gradb_ref, gradb_hbm, sems.at[3 * groups])
    store_grad.start()
    gram = nt_dot(gradb, gradb).astype(BF16)

    def put_packs(ref, side):
        for n in range(y_size):
            d = 2 * n + side
            i = d % half
            top = i * 128 + (64 if d >= half else 0)
            for k in range(half):
                j = (d + k) % blocks
                ref[n, count + k * 128 : count + (k + 1) * 128, :] = gram[d * 128 : (d + 1) * 128, j * 128 : (j + 1) * 128]
            ref[n, count + half * 128 :, :] = gram[top : top + 64, (i + half) * 128 : (i + half + 1) * 128]

    @pl.when(core == 0)
    def _():
        put_packs(own_ref, 0)
        put_packs(other_ref, 1)

    @pl.when(core != 0)
    def _():
        put_packs(own_ref, 1)
        put_packs(other_ref, 0)

    store_grad.wait()


def add_kernel(own_ref, other_ref, out_ref):
    out_ref[...] = (own_ref[...].astype(F32) + other_ref[...].astype(F32)).astype(BF16)


def return_kernel(part_ref, out_ref, pack_ref):
    experts = out_ref.shape[0]
    count = part_ref.shape[1] - pack_ref.shape[0]
    number = row_numbers(128)
    take = one_hot(jnp.where((number & 7) < 4, (number >> 3) * 4 + (number & 7), -1), lane_numbers(64))
    total = part_ref[0].astype(F32)
    for k in range(1, part_ref.shape[0]):
        total = total + part_ref[k].astype(F32)
    total = total.astype(BF16)
    pack_ref[...] = total[count:]
    out_ref[:, 0:16, :] = total[: experts * 16].reshape(experts, 16, 128)
    for s in range(experts // 16):
        left = nn_dot(take, total[experts * 16 + s * 64 : experts * 16 + (s + 1) * 64])
        out_ref[16 * s : 16 * (s + 1), 16:24, :] = left.reshape(16, 8, 128).astype(BF16)


def ortho_kernel(
    width, spot_ref, own_near_ref, own_far_ref, other_near_ref, other_far_ref, gradb_hbm, out_ref,
    gram_ref, pack_ref, gradb_ref, sem,
):
    fetch_grad = pltpu.make_async_copy(gradb_hbm, gradb_ref, sem)
    fetch_grad.start()
    blocks = gram_ref.shape[0] // 128
    half = blocks // 2
    squares = jnp.zeros((8, 128), F32)
    for i, ref in enumerate((own_near_ref, own_far_ref, other_near_ref, other_far_ref)):
        for k in range(2):
            pack = ref[k]
            pack_ref[2 * i + k] = pack
            square = pack.astype(F32)
            square = square * square
            squares = squares + 2.0 * jnp.sum(square.reshape(-1, 8, 128), axis=0)
            squares = squares - jnp.sum(square[:128].reshape(-1, 8, 128), axis=0)
    norm_sq = jnp.sqrt(jnp.sum(squares, keepdims=True)) + 1e-06
    for d in range(blocks):
        spot = spot_ref[d]
        rows = slice(d * 128, (d + 1) * 128)
        for k in range(half):
            lanes = slice((d + k) % blocks * 128, ((d + k) % blocks + 1) * 128)
            block = pack_ref[spot, k * 128 : (k + 1) * 128, :]
            gram_ref[rows, lanes] = block
            if k > 0:
                gram_ref[lanes, rows] = block.T
        i = d % half
        top = i * 128 + (64 if d >= half else 0)
        gram_ref[top : top + 64, (i + half) * 128 : (i + half + 1) * 128] = pack_ref[spot, half * 128 :, :]
    for i in range(half):
        upper = gram_ref[i * 128 : (i + 1) * 128, (i + half) * 128 : (i + half + 1) * 128]
        gram_ref[(i + half) * 128 : (i + half + 1) * 128, i * 128 : (i + 1) * 128] = upper.T

    inverse = 1.0 / norm_sq
    gram = gram_ref[...]
    fetch_grad.wait()
    first = (gradb_ref[...].astype(F32) * lax.rsqrt(norm_sq)).astype(BF16)

    def apply(value):
        return nn_dot(gram, value) * inverse

    second = (1.5 * first.astype(F32) - 0.5 * apply(first)).astype(BF16)
    power_one = apply(second).astype(BF16)
    power_two = apply(power_one).astype(BF16)
    power_three = apply(power_two)
    total = 1.5 * second.astype(F32)
    total = total - 0.5 * (2.25 * power_one.astype(F32) - 1.5 * power_two.astype(F32) + 0.25 * power_three)
    out_ref[0] = total * width**0.5


def in_hbm(value):
    return pltpu.with_memory_space_constraint(value, pltpu.HBM)


def whole(value):
    return pl.BlockSpec(value.shape, lambda *_: (0,) * len(value.shape))


def call(kernel, outs, ins, scratch=(), vmem=24, steps=(), specs=None, out_specs=None):
    specs = specs or {}
    out_specs = out_specs or {}
    flat, tree = jax.tree.flatten(outs)
    return pl.pallas_call(
        kernel,
        out_shape=outs,
        grid=steps,
        in_specs=[specs.get(i, whole(value)) for i, value in enumerate(ins)],
        out_specs=jax.tree.unflatten(tree, [out_specs.get(i, whole(value)) for i, value in enumerate(flat)]),
        scratch_shapes=list(scratch),
        compiler_params=pltpu.CompilerParams(vmem_limit_bytes=vmem * MIB),
    )(*ins)


def per_device(grad_out, hidden, gate_prob, expert_ids, weights):
    tokens, width_part = grad_out.shape
    top_count = expert_ids.shape[1]
    unit_part = hidden.shape[2]
    units = weights.shape[1]
    experts = lax.axis_size("x") * lax.axis_size("z")
    y_size = lax.axis_size("y")
    dp = y_size * 2
    width = width_part * dp
    capacity = 5 * tokens * top_count // (4 * experts)
    total_slots = experts * capacity
    pair_count = tokens * top_count
    y = lax.axis_index("y")
    c = lax.axis_index("c")
    block = jnp.arange(dp, dtype=jnp.int32)
    other_core = (block % 2) ^ c
    flip = y ^ (block // 2)
    pair_spot = other_core * y_size + (flip ^ (flip >> 1))
    came_from = other_core * y_size + (y - block // 2) % y_size
    core = jnp.full((1,), c)
    pair_spots = jnp.concatenate([pair_spot, core]).astype(jnp.int32)

    scaled_part = (gate_prob[:, :, None] * hidden.astype(F32)).astype(BF16)
    scaled_part = scaled_part.transpose(1, 0, 2).reshape(pair_count, unit_part)
    columns = width_part // 128

    def shape(*dims):
        return jax.ShapeDtypeStruct(dims, BF16)

    row = jax.ShapeDtypeStruct((1, pair_count), jnp.int32)
    sent_scaled, main_index, late_index, slot_index = call(
        send_scaled_kernel, (shape(experts, 24, 128), row, row, row), (expert_ids.T, scaled_part)
    )
    got_scaled = exchange(sent_scaled, EXPERT)
    got = exchange(
        call(send_grad_kernel, shape(experts, 20 * columns, 128), (main_index, late_index, grad_out)), EXPERT
    )

    scaled = call(unpack_kernel, shape(total_slots, unit_part), (got_scaled,), vmem=8)
    gathered = jnp.stack([scaled] + [shift_y(scaled, k, y_size) for k in range(1, y_size)])
    turned = call(
        turn_kernel, pltpu.HBM((units, total_slots), BF16), (came_from.astype(jnp.int32), gathered, swap_core(gathered)),
        specs={0: SMEM},
        vmem=20,
    )

    pack_rows = units // 2 + 64
    dp_parts = shape(y_size, total_slots + pack_rows, 128)
    groups = experts // 16
    own, other, grad_bf16 = call(
        core_kernel,
        (dp_parts, dp_parts, pltpu.HBM((units, width_part), BF16)),
        (pair_spots, in_hbm(got), in_hbm(weights[0]), in_hbm(turned)),
        (
            pltpu.VMEM((total_slots, width_part), BF16),
            pltpu.VMEM(got.shape, BF16),
            pltpu.VMEM((units, width_part), BF16),
            pltpu.VMEM((units, total_slots), BF16),
            pltpu.VMEM((units, width_part), BF16),
            pltpu.SemaphoreType.DMA((3 * groups + 1,)),
        ),
        specs={0: SMEM, 1: HBM, 2: HBM, 3: HBM},
        out_specs={2: HBM},
        vmem=32,
    )
    both = call(add_kernel, dp_parts, (own, swap_core(other)), vmem=12)
    parts = exchange(both, "y")
    sent_back, mine = call(
        return_kernel, (pltpu.HBM((experts, 24, 128), BF16), shape(pack_rows, 128)), (parts,), vmem=12
    )
    returned = exchange(sent_back, EXPERT).reshape(experts * 24, unit_part)
    chosen = (jnp.arange(experts * 24, dtype=jnp.int32)[:, None] == slot_index).astype(BF16)
    picked = lax.dot_general(chosen, returned, (((0,), (0,)), ((), ())), preferred_element_type=F32)
    picked = picked.reshape(top_count, tokens, unit_part).transpose(1, 0, 2)
    hidden_grad = (gate_prob[:, :, None] * picked).astype(BF16)

    near = jnp.stack([mine, swap_y(mine, 1, y_size)])
    far = swap_y(near, 3, y_size)
    update = call(
        lambda *refs: ortho_kernel(width, *refs),
        jax.ShapeDtypeStruct((1, units, width_part), F32),
        (pair_spots, near, far, swap_core(near), swap_core(far), in_hbm(grad_bf16)),
        (
            pltpu.VMEM((units, units), BF16),
            pltpu.VMEM((dp, units // 2 + 64, 128), BF16),
            pltpu.VMEM((units, width_part), BF16),
            pltpu.SemaphoreType.DMA,
        ),
        specs={0: SMEM, 5: HBM},
        vmem=32,
    )
    return (hidden_grad, update)


def solution(mesh):
    dp, experts = mesh.devices.shape
    x_size = 4
    split = Mesh(
        mesh.devices.reshape(dp // 2, 2, x_size, experts // x_size), ("y", "c", "x", "z")
    )
    rows, cols = ("x", "z"), ("y", "c")
    in_specs = (P(rows, cols), P(rows, None, cols), P(rows, None), P(rows, None), P(rows, None, cols))
    out_specs = (P(rows, None, cols), P(rows, None, cols))
    return jax.shard_map(per_device, mesh=split, in_specs=in_specs, out_specs=out_specs, check_vma=False)
```

```python
import jax
import jax.numpy as jnp
from jax import lax
from jax.experimental import pallas as pl
from jax.experimental.pallas import tpu as pltpu
from jax.sharding import Mesh, PartitionSpec as P

EXPERT = ("x", "z")
MIB = 1024 * 1024
BF16 = jnp.bfloat16
F32 = jnp.float32
SMEM = pl.BlockSpec(memory_space=pltpu.SMEM)
LOOSE = pl.BlockSpec(memory_space=pl.ANY)
HBM = pl.BlockSpec(memory_space=pltpu.HBM)


def shift_y(value, step, size):
    return lax.ppermute(value, "y", [(i, (i + step) % size) for i in range(size)])


def swap_y(value, flip, size):
    return lax.ppermute(value, "y", [(i, i ^ flip) for i in range(size)])


def swap_core(value):
    return lax.ppermute(value, "c", [(0, 1), (1, 0)])


def exchange(value, axes):
    return lax.all_to_all(value, axes, split_axis=0, concat_axis=0, tiled=True)


def nt_dot(left, right):
    return lax.dot_general(left, right, (((1,), (1,)), ((), ())), preferred_element_type=F32)


def nn_dot(left, right):
    return jnp.dot(left, right, preferred_element_type=F32)


def one_hot(rows, index):
    return jnp.where(rows == index, 1.0, 0.0).astype(BF16)


def row_numbers(count):
    return lax.broadcasted_iota(jnp.int32, (count, 1), 0)


def lane_numbers(count):
    return lax.broadcasted_iota(jnp.int32, (1, count), 1)


def fetch(source, target, size, sems, first):
    copies = []
    for s in range(source.shape[0] // size):
        here = slice(s * size, (s + 1) * size)
        copies.append(pltpu.make_async_copy(source.at[here], target.at[here], sems.at[first + s]))
        copies[-1].start()
    return copies


def send_kernel(ids_ref, scaled_ref, grad_ref, out_ref, slot_ref):
    experts, height, _ = out_ref.shape
    count, tokens = ids_ref.shape
    blocks = grad_ref.shape[1] // 128
    main = 16 * (blocks + 1)
    tail = height - main
    earlier = jnp.where(row_numbers(tokens) < lane_numbers(tokens), 1.0, 0.0).astype(BF16)
    passed = jnp.zeros((experts, 1), F32)
    ids, ranks = [], []
    for k in range(count):
        ids.append(ids_ref[k : k + 1, :])
        named = one_hot(row_numbers(experts), ids[k])
        wide = named.astype(F32)
        before = nn_dot(named, earlier) + passed
        ranks.append(jnp.sum(wide * before, axis=0, keepdims=True).astype(jnp.int32))
        passed = passed + jnp.sum(wide, axis=1, keepdims=True)
    owner = jnp.concatenate(ids, axis=1)
    rank = jnp.concatenate(ranks, axis=1)
    late = rank >= 16
    slot_ref[...] = owner * 24 + rank

    scaled = scaled_ref[...]
    grad = grad_ref[...]
    chosen = one_hot(row_numbers(experts * 16), jnp.where(late, -1, owner * 16 + rank))
    part = nn_dot(chosen, scaled).astype(BF16)
    out_ref[:, 0:16, :] = part.reshape(experts, 16, 128)
    rows = nn_dot(chosen[:, :tokens] + chosen[:, tokens:], grad).astype(BF16)
    for b in range(blocks):
        out_ref[:, 16 * (b + 1) : 16 * (b + 2), :] = rows[:, b * 128 : (b + 1) * 128].reshape(experts, 16, 128)
    expert = lax.broadcasted_iota(jnp.int32, (experts, tail, 1), 0)
    place = lax.broadcasted_iota(jnp.int32, (experts, tail, 1), 1)
    number = (expert * tail + (place & 3)).reshape(experts * tail, 1)
    kind = (place >> 2).reshape(experts * tail, 1)
    chosen = one_hot(number, jnp.where(late, owner * tail + rank - 16, -1))
    part = nn_dot(chosen, scaled)
    total = jnp.where(kind == 0, part, 0.0)
    rows = nn_dot(chosen[:, :tokens] + chosen[:, tokens:], grad)
    for b in range(blocks):
        total = jnp.where(kind == b + 1, rows[:, b * 128 : (b + 1) * 128], total)
    out_ref[:, main:, :] = total.reshape(experts, tail, 128).astype(BF16)


def late_rows(got_ref, main, s, kinds):
    tail = got_ref.shape[1] - main
    group = got_ref[8 * s : 8 * (s + 1), main:, :].astype(F32).reshape(8 * tail, 128).astype(BF16)
    number = row_numbers(32 * kinds)
    order = one_hot(((number >> 2) & 7) * tail + (number >> 5) * 4 + (number & 3), lane_numbers(8 * tail))
    return nn_dot(order, group).astype(BF16)


def unpack_kernel(got_ref, out_hbm, scaled_ref, sems):
    experts, height, _ = got_ref.shape
    main = (height // 16 - 1) * 16
    scaled_ref[: experts * 16] = got_ref[:, 0:16, :].reshape(experts * 16, 128)
    for s in range(experts // 8):
        scaled_ref[experts * 16 + 32 * s : experts * 16 + 32 * (s + 1)] = late_rows(got_ref, main, s, 1)
    copies = []
    for k in range(out_hbm.shape[0]):
        copies.append(pltpu.make_async_copy(scaled_ref, out_hbm.at[k], sems.at[k]))
        copies[-1].start()
    for copy in copies:
        copy.wait()


def back_kernel(
    spot_ref, got_ref, weight_hbm, own_hbm, other_ref, rows_hbm, own_ref, rows_ref, weight_ref, sems
):
    experts, height, _ = got_ref.shape
    columns = rows_ref.shape[1] // 128
    blocks = weight_ref.shape[0] // 128
    y_size = blocks // 2
    main = 16 * (columns + 1)
    fetch_weight = fetch(weight_hbm, weight_ref, weight_ref.shape[0] // y_size, sems, 0)
    for b in range(columns):
        lanes = slice(b * 128, (b + 1) * 128)
        rows_ref[: experts * 16, lanes] = got_ref[:, 16 * (b + 1) : 16 * (b + 2), :].reshape(experts * 16, 128)
    for s in range(experts // 8):
        late = late_rows(got_ref, main, s, columns + 1)
        for b in range(columns):
            rows_ref[experts * 16 + 32 * s : experts * 16 + 32 * (s + 1), b * 128 : (b + 1) * 128] = late[
                32 * (b + 1) : 32 * (b + 2)
            ]
    store_rows = pltpu.make_async_copy(rows_ref, rows_hbm, sems.at[y_size])
    store_rows.start()
    for copy in fetch_weight:
        copy.wait()
    term = nt_dot(rows_ref[...], weight_ref[...]).astype(BF16)
    core = spot_ref[blocks]

    def put_terms(own, other):
        for k in range(y_size):
            own_ref[k] = term[:, (2 * k + own) * 128 : (2 * k + own + 1) * 128]
            other_ref[k] = term[:, (2 * k + other) * 128 : (2 * k + other + 1) * 128]

    @pl.when(core == 0)
    def _():
        put_terms(0, 1)

    @pl.when(core != 0)
    def _():
        put_terms(1, 0)

    stores = fetch(own_ref, own_hbm, 1, sems, y_size + 1)
    for copy in stores:
        copy.wait()
    store_rows.wait()


def grad_kernel(
    spot_ref, own_hbm, other_hbm, rows_hbm, gradb_hbm, pack_own_ref, pack_other_ref,
    own_ref, other_ref, rows_ref, wide_ref, gradb_ref, sems,
):
    blocks = gradb_ref.shape[0] // 128
    y_size = blocks // 2
    half = blocks // 2
    copies = fetch(own_hbm, own_ref, 1, sems, 0)
    copies += fetch(other_hbm, other_ref, 1, sems, y_size)
    copies += fetch(rows_hbm, rows_ref, rows_ref.shape[0] // y_size, sems, 2 * y_size)
    for copy in copies:
        copy.wait()
    core = spot_ref[blocks]

    def put_units(ref, side):
        for n in range(y_size):
            wide_ref[:, (2 * n + side) * 128 : (2 * n + side + 1) * 128] = ref[n]

    @pl.when(core == 0)
    def _():
        put_units(own_ref, 0)
        put_units(other_ref, 1)

    @pl.when(core != 0)
    def _():
        put_units(own_ref, 1)
        put_units(other_ref, 0)

    gradb = lax.dot_general(
        wide_ref[...], rows_ref[...], (((0,), (0,)), ((), ())), preferred_element_type=F32
    ).astype(BF16)
    gradb_ref[...] = gradb
    store_grad = pltpu.make_async_copy(gradb_ref, gradb_hbm, sems.at[3 * y_size])
    store_grad.start()
    gram = nt_dot(gradb, gradb).astype(BF16)

    def put_packs(ref, side):
        for n in range(y_size):
            d = 2 * n + side
            i = d % half
            top = i * 128 + (64 if d >= half else 0)
            for k in range(half):
                j = (d + k) % blocks
                ref[n, k * 128 : (k + 1) * 128, :] = gram[d * 128 : (d + 1) * 128, j * 128 : (j + 1) * 128]
            ref[n, half * 128 :, :] = gram[top : top + 64, (i + half) * 128 : (i + half + 1) * 128]

    @pl.when(core == 0)
    def _():
        put_packs(pack_own_ref, 0)
        put_packs(pack_other_ref, 1)

    @pl.when(core != 0)
    def _():
        put_packs(pack_own_ref, 1)
        put_packs(pack_other_ref, 0)

    store_grad.wait()


def add_kernel(own_ref, other_ref, after_ref, out_ref):
    out_ref[...] = (own_ref[...].astype(F32) + other_ref[...].astype(F32)).astype(BF16)


def sum_parts(part_ref):
    total = part_ref[0].astype(F32)
    for k in range(1, part_ref.shape[0]):
        total = total + part_ref[k].astype(F32)
    return total.astype(BF16)


def return_kernel(part_ref, pack_part_ref, out_ref, pack_ref):
    experts = out_ref.shape[0]
    number = row_numbers(128)
    take = one_hot(jnp.where((number & 7) < 4, (number >> 3) * 4 + (number & 7), -1), lane_numbers(64))
    pack_ref[...] = sum_parts(pack_part_ref)
    total = sum_parts(part_ref)
    out_ref[:, 0:16, :] = total[: experts * 16].reshape(experts, 16, 128)
    for s in range(experts // 16):
        left = nn_dot(take, total[experts * 16 + s * 64 : experts * 16 + (s + 1) * 64])
        out_ref[16 * s : 16 * (s + 1), 16:24, :] = left.reshape(16, 8, 128).astype(BF16)


def ortho_kernel(
    width, spot_ref, own_near_ref, own_far_ref, other_near_ref, other_far_ref, gradb_hbm, out_ref,
    gram_ref, pack_ref, gradb_ref, sem,
):
    fetch_grad = pltpu.make_async_copy(gradb_hbm, gradb_ref, sem)
    fetch_grad.start()
    blocks = gram_ref.shape[0] // 128
    half = blocks // 2
    squares = jnp.zeros((8, 128), F32)
    for i, ref in enumerate((own_near_ref, own_far_ref, other_near_ref, other_far_ref)):
        for k in range(2):
            pack = ref[k]
            pack_ref[2 * i + k] = pack
            square = pack.astype(F32)
            square = square * square
            squares = squares + 2.0 * jnp.sum(square.reshape(-1, 8, 128), axis=0)
            squares = squares - jnp.sum(square[:128].reshape(-1, 8, 128), axis=0)
    norm_sq = jnp.sqrt(jnp.sum(squares, keepdims=True)) + 1e-06
    for d in range(blocks):
        spot = spot_ref[d]
        rows = slice(d * 128, (d + 1) * 128)
        for k in range(half):
            lanes = slice((d + k) % blocks * 128, ((d + k) % blocks + 1) * 128)
            block = pack_ref[spot, k * 128 : (k + 1) * 128, :]
            gram_ref[rows, lanes] = block
            if k > 0:
                gram_ref[lanes, rows] = block.T
        i = d % half
        top = i * 128 + (64 if d >= half else 0)
        gram_ref[top : top + 64, (i + half) * 128 : (i + half + 1) * 128] = pack_ref[spot, half * 128 :, :]
    for i in range(half):
        upper = gram_ref[i * 128 : (i + 1) * 128, (i + half) * 128 : (i + half + 1) * 128]
        gram_ref[(i + half) * 128 : (i + half + 1) * 128, i * 128 : (i + 1) * 128] = upper.T

    inverse = 1.0 / norm_sq
    gram = gram_ref[...]
    fetch_grad.wait()
    first = (gradb_ref[...].astype(F32) * lax.rsqrt(norm_sq)).astype(BF16)

    def apply(value):
        return nn_dot(gram, value) * inverse

    second = (1.5 * first.astype(F32) - 0.5 * apply(first)).astype(BF16)
    power_one = apply(second).astype(BF16)
    power_two = apply(power_one).astype(BF16)
    power_three = apply(power_two)
    total = 1.5 * second.astype(F32)
    total = total - 0.5 * (2.25 * power_one.astype(F32) - 1.5 * power_two.astype(F32) + 0.25 * power_three)
    out_ref[0] = total * width**0.5


def in_hbm(value):
    return pltpu.with_memory_space_constraint(value, pltpu.HBM)


def whole(value):
    return pl.BlockSpec(value.shape, lambda *_: (0,) * len(value.shape))


def call(kernel, outs, ins, scratch=(), vmem=24, steps=(), specs=None, out_specs=None):
    specs = specs or {}
    out_specs = out_specs or {}
    flat, tree = jax.tree.flatten(outs)
    return pl.pallas_call(
        kernel,
        out_shape=outs,
        grid=steps,
        in_specs=[specs.get(i, whole(value)) for i, value in enumerate(ins)],
        out_specs=jax.tree.unflatten(tree, [out_specs.get(i, whole(value)) for i, value in enumerate(flat)]),
        scratch_shapes=list(scratch),
        compiler_params=pltpu.CompilerParams(vmem_limit_bytes=vmem * MIB),
    )(*ins)


def per_device(grad_out, hidden, gate_prob, expert_ids, weights):
    tokens, width_part = grad_out.shape
    top_count = expert_ids.shape[1]
    unit_part = hidden.shape[2]
    units = weights.shape[1]
    experts = lax.axis_size("x") * lax.axis_size("z")
    y_size = lax.axis_size("y")
    dp = y_size * 2
    width = width_part * dp
    capacity = 5 * tokens * top_count // (4 * experts)
    total_slots = experts * capacity
    pair_count = tokens * top_count
    y = lax.axis_index("y")
    c = lax.axis_index("c")
    block = jnp.arange(dp, dtype=jnp.int32)
    other_core = (block % 2) ^ c
    flip = y ^ (block // 2)
    pair_spot = other_core * y_size + (flip ^ (flip >> 1))
    core = jnp.full((1,), c)
    pair_spots = jnp.concatenate([pair_spot, core]).astype(jnp.int32)

    scaled_part = (gate_prob[:, :, None] * hidden.astype(F32)).astype(BF16)
    scaled_part = scaled_part.transpose(1, 0, 2).reshape(pair_count, unit_part)
    columns = width_part // 128
    main_rows = 16 * (columns + 1)
    tail = -(-4 * (columns + 1) // 8) * 8

    def shape(*dims):
        return jax.ShapeDtypeStruct(dims, BF16)

    sent, slot_index = call(
        send_kernel,
        (shape(experts, main_rows + tail, 128), jax.ShapeDtypeStruct((1, pair_count), jnp.int32)),
        (expert_ids.T, scaled_part, grad_out),
    )
    got = exchange(sent, EXPERT)

    parts_shape = (y_size, total_slots, unit_part)
    gathered = exchange(
        call(
            unpack_kernel,
            pltpu.HBM(parts_shape, BF16),
            (got,),
            (pltpu.VMEM((total_slots, unit_part), BF16), pltpu.SemaphoreType.DMA((y_size,))),
            out_specs={0: HBM},
            vmem=12,
        ),
        "y",
    )
    gathered_other = swap_core(gathered)
    term_own, term_other, rows = call(
        back_kernel,
        (pltpu.HBM(parts_shape, BF16), shape(*parts_shape), pltpu.HBM((total_slots, width_part), BF16)),
        (pair_spots, got, in_hbm(weights[0])),
        (
            pltpu.VMEM(parts_shape, BF16),
            pltpu.VMEM((total_slots, width_part), BF16),
            pltpu.VMEM((units, width_part), BF16),
            pltpu.SemaphoreType.DMA((2 * y_size + 1,)),
        ),
        specs={0: SMEM, 2: HBM},
        out_specs={0: HBM, 2: HBM},
        vmem=24,
    )

    def piece(count):
        return pl.BlockSpec((1, count, 128), lambda i: (i, 0, 0))

    both = call(
        add_kernel,
        pltpu.HBM(parts_shape, BF16),
        (in_hbm(term_own), swap_core(term_other), gathered),
        steps=(y_size,),
        specs={0: piece(total_slots), 1: piece(total_slots), 2: LOOSE},
        out_specs={0: piece(total_slots)},
        vmem=8,
    )
    parts = exchange(both, "y")

    pack_rows = units // 2 + 64
    packs = shape(y_size, pack_rows, 128)
    grad_bf16, pack_own, pack_other = call(
        grad_kernel,
        (pltpu.HBM((units, width_part), BF16), packs, packs),
        (pair_spots, in_hbm(gathered), in_hbm(gathered_other), in_hbm(rows)),
        (
            pltpu.VMEM(parts_shape, BF16),
            pltpu.VMEM(parts_shape, BF16),
            pltpu.VMEM((total_slots, width_part), BF16),
            pltpu.VMEM((total_slots, units), BF16),
            pltpu.VMEM((units, width_part), BF16),
            pltpu.SemaphoreType.DMA((3 * y_size + 1,)),
        ),
        specs={0: SMEM, 1: HBM, 2: HBM, 3: HBM},
        out_specs={0: HBM},
        vmem=32,
    )
    pack_both = call(add_kernel, packs, (pack_own, swap_core(pack_other), parts), specs={2: LOOSE}, vmem=8)
    pack_parts = exchange(pack_both, "y")
    sent_back, mine = call(
        return_kernel,
        (pltpu.HBM((experts, 24, 128), BF16), shape(pack_rows, 128)),
        (parts, pack_parts),
        vmem=12,
    )
    returned = exchange(sent_back, EXPERT).reshape(experts * 24, unit_part)
    chosen = (jnp.arange(experts * 24, dtype=jnp.int32)[:, None] == slot_index).astype(BF16)
    picked = lax.dot_general(chosen, returned, (((0,), (0,)), ((), ())), preferred_element_type=F32)
    picked = picked.reshape(top_count, tokens, unit_part).transpose(1, 0, 2)
    hidden_grad = (gate_prob[:, :, None] * picked).astype(BF16)

    near = jnp.stack([mine, swap_y(mine, 1, y_size)])
    far = swap_y(near, 3, y_size)
    update = call(
        lambda *refs: ortho_kernel(width, *refs),
        jax.ShapeDtypeStruct((1, units, width_part), F32),
        (pair_spots, near, far, swap_core(near), swap_core(far), in_hbm(grad_bf16)),
        (
            pltpu.VMEM((units, units), BF16),
            pltpu.VMEM((dp, units // 2 + 64, 128), BF16),
            pltpu.VMEM((units, width_part), BF16),
            pltpu.SemaphoreType.DMA,
        ),
        specs={0: SMEM, 5: HBM},
        vmem=32,
    )
    return (hidden_grad, update)


def solution(mesh):
    dp, experts = mesh.devices.shape
    x_size = 4
    split = Mesh(
        mesh.devices.reshape(dp // 2, 2, x_size, experts // x_size), ("y", "c", "x", "z")
    )
    rows, cols = ("x", "z"), ("y", "c")
    in_specs = (P(rows, cols), P(rows, None, cols), P(rows, None), P(rows, None), P(rows, None, cols))
    out_specs = (P(rows, None, cols), P(rows, None, cols))
    return jax.shard_map(per_device, mesh=split, in_specs=in_specs, out_specs=out_specs, check_vma=False)
```

```python
import jax
import jax.numpy as jnp
from jax import lax
from jax.experimental import pallas as pl
from jax.experimental.pallas import tpu as pltpu
from jax.sharding import Mesh, PartitionSpec as P

EXPERT = ("x", "z")
MIB = 1024 * 1024
BF16 = jnp.bfloat16
F32 = jnp.float32
SMEM = pl.BlockSpec(memory_space=pltpu.SMEM)
LOOSE = pl.BlockSpec(memory_space=pl.ANY)
HBM = pl.BlockSpec(memory_space=pltpu.HBM)


def shift_y(value, step, size):
    return lax.ppermute(value, "y", [(i, (i + step) % size) for i in range(size)])


def swap_y(value, flip, size):
    return lax.ppermute(value, "y", [(i, i ^ flip) for i in range(size)])


def swap_core(value):
    return lax.ppermute(value, "c", [(0, 1), (1, 0)])


def exchange(value, axes):
    return lax.all_to_all(value, axes, split_axis=0, concat_axis=0, tiled=True)


def nt_dot(left, right):
    return lax.dot_general(left, right, (((1,), (1,)), ((), ())), preferred_element_type=F32)


def nn_dot(left, right):
    return jnp.dot(left, right, preferred_element_type=F32)


def one_hot(rows, index):
    return jnp.where(rows == index, 1.0, 0.0).astype(BF16)


def row_numbers(count):
    return lax.broadcasted_iota(jnp.int32, (count, 1), 0)


def lane_numbers(count):
    return lax.broadcasted_iota(jnp.int32, (1, count), 1)


def send_scaled_kernel(ids_ref, scaled_ref, out_ref, main_ref, late_ref, slot_ref):
    experts = out_ref.shape[0]
    count, tokens = ids_ref.shape
    earlier = jnp.where(row_numbers(tokens) < lane_numbers(tokens), 1.0, 0.0).astype(BF16)
    passed = jnp.zeros((experts, 1), F32)
    ids, ranks = [], []
    for k in range(count):
        ids.append(ids_ref[k : k + 1, :])
        named = one_hot(row_numbers(experts), ids[k])
        wide = named.astype(F32)
        before = nn_dot(named, earlier) + passed
        ranks.append(jnp.sum(wide * before, axis=0, keepdims=True).astype(jnp.int32))
        passed = passed + jnp.sum(wide, axis=1, keepdims=True)
    expert = jnp.concatenate(ids, axis=1)
    rank = jnp.concatenate(ranks, axis=1)
    late = rank >= 16
    main_index = jnp.where(late, -1, expert * 16 + rank)
    main_ref[...] = main_index
    late_ref[...] = jnp.where(late, expert * 16 + rank - 16, -1)
    slot_ref[...] = expert * 24 + rank
    left_index = jnp.where(late, expert * 8 + rank - 16, -1)
    scaled = scaled_ref[...]
    part = nn_dot(one_hot(row_numbers(experts * 16), main_index), scaled).astype(BF16)
    out_ref[:, 0:16, :] = part.reshape(experts, 16, 128)
    part = nn_dot(one_hot(row_numbers(experts * 8), left_index), scaled)
    out_ref[:, 16:24, :] = part.reshape(experts, 8, 128).astype(BF16)


def send_grad_kernel(main_ref, late_ref, grad_ref, out_ref):
    experts = out_ref.shape[0]
    tokens, width_part = grad_ref.shape
    blocks = width_part // 128
    grad = grad_ref[...]
    chosen = one_hot(row_numbers(experts * 16), main_ref[...])
    rows = nn_dot(chosen[:, :tokens] + chosen[:, tokens:], grad).astype(BF16)
    for b in range(blocks):
        out_ref[:, 16 * b : 16 * (b + 1), :] = rows[:, b * 128 : (b + 1) * 128].reshape(experts, 16, 128)
    number = row_numbers(experts * 16)
    chosen = one_hot((number & -16) + (number & 3), late_ref[...])
    rows = nn_dot(chosen[:, :tokens] + chosen[:, tokens:], grad)
    column = (number >> 2) & 3
    total = rows[:, 0:128]
    for b in range(1, blocks):
        total = jnp.where(column == b, rows[:, b * 128 : (b + 1) * 128], total)
    out_ref[:, 16 * blocks :, :] = total.astype(BF16).reshape(experts, 16, 128)


def unpack_kernel(got_ref, out_ref):
    experts = got_ref.shape[0]
    out_ref[: experts * 16] = got_ref[:, 0:16, :].reshape(experts * 16, 128)
    tail = got_ref[:, 16:24, :].astype(F32).reshape(experts * 8, 128).astype(BF16)
    number = row_numbers(experts * 4)
    take = one_hot((number >> 2) * 8 + (number & 3), lane_numbers(experts * 8))
    out_ref[experts * 16 :] = nn_dot(take, tail).astype(BF16)


def turn_kernel(spot_ref, own_ref, other_ref, out_ref):
    blocks = out_ref.shape[0] // 128
    y_size = blocks // 2
    for d in range(blocks):
        spot = spot_ref[d]

        @pl.when(spot < y_size)
        def _():
            out_ref[d * 128 : (d + 1) * 128, :] = own_ref[spot].T

        @pl.when(spot >= y_size)
        def _():
            out_ref[d * 128 : (d + 1) * 128, :] = other_ref[spot - y_size].T


def core_kernel(
    spot_ref, got_hbm, weight_hbm, turned_hbm,
    own_ref, other_ref, gradb_hbm,
    rows_ref, got_ref, weight_ref, turned_ref, gradb_ref, sems,
):
    experts = got_ref.shape[0]
    columns = rows_ref.shape[1] // 128
    blocks = weight_ref.shape[0] // 128
    y_size = blocks // 2
    half = blocks // 2
    groups = experts // 16
    part = weight_ref.shape[0] // groups

    def fetch(source, target, size, first):
        copies = []
        for s in range(groups):
            here = slice(s * size, (s + 1) * size)
            copies.append(pltpu.make_async_copy(source.at[here], target.at[here], sems.at[first + s]))
            copies[-1].start()
        return copies

    fetch_got = fetch(got_hbm, got_ref, 16, 0)
    fetch_weight = fetch(weight_hbm, weight_ref, part, groups)

    number = row_numbers(256)
    order = one_hot(((number >> 2) & 15) * 16 + (number >> 6) * 4 + (number & 3), lane_numbers(256))
    for s in range(groups):
        fetch_got[s].wait()
        here = slice(16 * s, 16 * (s + 1))
        late = nn_dot(order, got_ref[here, 16 * columns :, :].reshape(256, 128)).astype(BF16)
        for b in range(columns):
            lanes = slice(b * 128, (b + 1) * 128)
            rows_ref[256 * s : 256 * (s + 1), lanes] = got_ref[here, 16 * b : 16 * (b + 1), :].reshape(256, 128)
            rows_ref[experts * 16 + s * 64 : experts * 16 + (s + 1) * 64, lanes] = late[b * 64 : (b + 1) * 64]
    fetch_turned = fetch(turned_hbm, turned_ref, part, 2 * groups)
    rows = rows_ref[...]
    core = spot_ref[blocks]
    count = rows_ref.shape[0]

    for copy in fetch_weight:
        copy.wait()
    term = nt_dot(rows, weight_ref[...]).astype(BF16)

    def put_terms(own, other):
        for k in range(y_size):
            own_ref[k, :count] = term[:, (2 * k + own) * 128 : (2 * k + own + 1) * 128]
            other_ref[k, :count] = term[:, (2 * k + other) * 128 : (2 * k + other + 1) * 128]

    @pl.when(core == 0)
    def _():
        put_terms(0, 1)

    @pl.when(core != 0)
    def _():
        put_terms(1, 0)

    for copy in fetch_turned:
        copy.wait()
    gradb = nn_dot(turned_ref[...], rows).astype(BF16)
    gradb_ref[...] = gradb
    store_grad = pltpu.make_async_copy(gradb_ref, gradb_hbm, sems.at[3 * groups])
    store_grad.start()
    gram = nt_dot(gradb, gradb).astype(BF16)

    def put_packs(ref, side):
        for n in range(y_size):
            d = 2 * n + side
            i = d % half
            top = i * 128 + (64 if d >= half else 0)
            for k in range(half):
                j = (d + k) % blocks
                ref[n, count + k * 128 : count + (k + 1) * 128, :] = gram[d * 128 : (d + 1) * 128, j * 128 : (j + 1) * 128]
            ref[n, count + half * 128 :, :] = gram[top : top + 64, (i + half) * 128 : (i + half + 1) * 128]

    @pl.when(core == 0)
    def _():
        put_packs(own_ref, 0)
        put_packs(other_ref, 1)

    @pl.when(core != 0)
    def _():
        put_packs(own_ref, 1)
        put_packs(other_ref, 0)

    store_grad.wait()


def add_kernel(own_ref, other_ref, out_ref):
    out_ref[...] = (own_ref[...].astype(F32) + other_ref[...].astype(F32)).astype(BF16)


def store_pieces(source, target, count, sems):
    size = source.shape[0] // count
    copies = []
    for k in range(count):
        piece = slice(k * size, (k + 1) * size)
        copies.append(pltpu.make_async_copy(source.at[piece], target.at[piece], sems.at[k]))
        copies[-1].start()
    for copy in copies:
        copy.wait()


def return_kernel(part_ref, out_hbm, pack_ref, out_ref, sems):
    experts = out_ref.shape[0]
    count = part_ref.shape[1] - pack_ref.shape[0]
    number = row_numbers(128)
    take = one_hot(jnp.where((number & 7) < 4, (number >> 3) * 4 + (number & 7), -1), lane_numbers(64))
    total = part_ref[0].astype(F32)
    for k in range(1, part_ref.shape[0]):
        total = total + part_ref[k].astype(F32)
    total = total.astype(BF16)
    pack_ref[...] = total[count:]
    out_ref[:, 0:16, :] = total[: experts * 16].reshape(experts, 16, 128)
    for s in range(experts // 16):
        left = nn_dot(take, total[experts * 16 + s * 64 : experts * 16 + (s + 1) * 64])
        out_ref[16 * s : 16 * (s + 1), 16:24, :] = left.reshape(16, 8, 128).astype(BF16)
    store_pieces(out_ref, out_hbm, 4, sems)


def ortho_kernel(
    width, spot_ref, own_near_ref, own_far_ref, other_near_ref, other_far_ref, gradb_hbm, out_hbm,
    gram_ref, pack_ref, gradb_ref, out_ref, sem, sems,
):
    fetch_grad = pltpu.make_async_copy(gradb_hbm, gradb_ref, sem)
    fetch_grad.start()
    blocks = gram_ref.shape[0] // 128
    half = blocks // 2
    squares = jnp.zeros((8, 128), F32)
    for i, ref in enumerate((own_near_ref, own_far_ref, other_near_ref, other_far_ref)):
        for k in range(2):
            pack = ref[k]
            pack_ref[2 * i + k] = pack
            square = pack.astype(F32)
            square = square * square
            squares = squares + 2.0 * jnp.sum(square.reshape(-1, 8, 128), axis=0)
            squares = squares - jnp.sum(square[:128].reshape(-1, 8, 128), axis=0)
    norm_sq = jnp.sqrt(jnp.sum(squares, keepdims=True)) + 1e-06
    for d in range(blocks):
        spot = spot_ref[d]
        rows = slice(d * 128, (d + 1) * 128)
        for k in range(half):
            lanes = slice((d + k) % blocks * 128, ((d + k) % blocks + 1) * 128)
            block = pack_ref[spot, k * 128 : (k + 1) * 128, :]
            gram_ref[rows, lanes] = block
            if k > 0:
                gram_ref[lanes, rows] = block.T
        i = d % half
        top = i * 128 + (64 if d >= half else 0)
        gram_ref[top : top + 64, (i + half) * 128 : (i + half + 1) * 128] = pack_ref[spot, half * 128 :, :]
    for i in range(half):
        upper = gram_ref[i * 128 : (i + 1) * 128, (i + half) * 128 : (i + half + 1) * 128]
        gram_ref[(i + half) * 128 : (i + half + 1) * 128, i * 128 : (i + 1) * 128] = upper.T

    inverse = 1.0 / norm_sq
    gram = gram_ref[...]
    fetch_grad.wait()
    first = (gradb_ref[...].astype(F32) * lax.rsqrt(norm_sq)).astype(BF16)

    def apply(value):
        return nn_dot(gram, value) * inverse

    second = (1.5 * first.astype(F32) - 0.5 * apply(first)).astype(BF16)
    power_one = apply(second).astype(BF16)
    power_two = apply(power_one).astype(BF16)
    near_terms = 1.5 * second.astype(F32) - 0.5 * (2.25 * power_one.astype(F32) - 1.5 * power_two.astype(F32))
    size = gram.shape[0] // 2
    part = size // 2
    stores = []
    for h in range(2):
        rows = slice(h * size, (h + 1) * size)
        power_three = nn_dot(gram[rows], power_two) * inverse
        out_ref[rows] = (near_terms[rows] - 0.125 * power_three) * width**0.5
        for q in range(2):
            piece = slice(h * size + q * part, h * size + (q + 1) * part)
            stores.append(pltpu.make_async_copy(out_ref.at[piece], out_hbm.at[0, piece], sems.at[2 * h + q]))
            stores[-1].start()
    for copy in stores:
        copy.wait()


def in_hbm(value):
    return pltpu.with_memory_space_constraint(value, pltpu.HBM)


def whole(value):
    return pl.BlockSpec(value.shape, lambda *_: (0,) * len(value.shape))


def call(kernel, outs, ins, scratch=(), vmem=24, steps=(), specs=None, out_specs=None):
    specs = specs or {}
    out_specs = out_specs or {}
    flat, tree = jax.tree.flatten(outs)
    return pl.pallas_call(
        kernel,
        out_shape=outs,
        grid=steps,
        in_specs=[specs.get(i, whole(value)) for i, value in enumerate(ins)],
        out_specs=jax.tree.unflatten(tree, [out_specs.get(i, whole(value)) for i, value in enumerate(flat)]),
        scratch_shapes=list(scratch),
        compiler_params=pltpu.CompilerParams(vmem_limit_bytes=vmem * MIB),
    )(*ins)


def per_device(grad_out, hidden, gate_prob, expert_ids, weights):
    tokens, width_part = grad_out.shape
    top_count = expert_ids.shape[1]
    unit_part = hidden.shape[2]
    units = weights.shape[1]
    experts = lax.axis_size("x") * lax.axis_size("z")
    y_size = lax.axis_size("y")
    dp = y_size * 2
    width = width_part * dp
    capacity = 5 * tokens * top_count // (4 * experts)
    total_slots = experts * capacity
    pair_count = tokens * top_count
    y = lax.axis_index("y")
    c = lax.axis_index("c")
    block = jnp.arange(dp, dtype=jnp.int32)
    other_core = (block % 2) ^ c
    flip = y ^ (block // 2)
    pair_spot = other_core * y_size + (flip ^ (flip >> 1))
    came_from = other_core * y_size + (y - block // 2) % y_size
    core = jnp.full((1,), c)
    pair_spots = jnp.concatenate([pair_spot, core]).astype(jnp.int32)

    scaled_part = (gate_prob[:, :, None] * hidden.astype(F32)).astype(BF16)
    scaled_part = scaled_part.transpose(1, 0, 2).reshape(pair_count, unit_part)
    columns = width_part // 128

    def shape(*dims):
        return jax.ShapeDtypeStruct(dims, BF16)

    row = jax.ShapeDtypeStruct((1, pair_count), jnp.int32)
    sent_scaled, main_index, late_index, slot_index = call(
        send_scaled_kernel, (shape(experts, 24, 128), row, row, row), (expert_ids.T, scaled_part)
    )
    got_scaled = exchange(sent_scaled, EXPERT)
    got = exchange(
        call(send_grad_kernel, shape(experts, 20 * columns, 128), (main_index, late_index, grad_out)), EXPERT
    )

    scaled = call(unpack_kernel, shape(total_slots, unit_part), (got_scaled,), vmem=8)
    gathered = jnp.stack([scaled] + [shift_y(scaled, k, y_size) for k in range(1, y_size)])
    turned = call(
        turn_kernel, pltpu.HBM((units, total_slots), BF16), (came_from.astype(jnp.int32), gathered, swap_core(gathered)),
        specs={0: SMEM},
        vmem=20,
    )

    pack_rows = units // 2 + 64
    dp_parts = shape(y_size, total_slots + pack_rows, 128)
    groups = experts // 16
    own, other, grad_bf16 = call(
        core_kernel,
        (dp_parts, dp_parts, pltpu.HBM((units, width_part), BF16)),
        (pair_spots, in_hbm(got), in_hbm(weights[0]), in_hbm(turned)),
        (
            pltpu.VMEM((total_slots, width_part), BF16),
            pltpu.VMEM(got.shape, BF16),
            pltpu.VMEM((units, width_part), BF16),
            pltpu.VMEM((units, total_slots), BF16),
            pltpu.VMEM((units, width_part), BF16),
            pltpu.SemaphoreType.DMA((3 * groups + 1,)),
        ),
        specs={0: SMEM, 1: HBM, 2: HBM, 3: HBM},
        out_specs={2: HBM},
        vmem=32,
    )
    both = call(add_kernel, dp_parts, (own, swap_core(other)), vmem=12)
    parts = exchange(both, "y")
    sent_back, mine = call(
        return_kernel,
        (pltpu.HBM((experts, 24, 128), BF16), shape(pack_rows, 128)),
        (parts,),
        (pltpu.VMEM((experts, 24, 128), BF16), pltpu.SemaphoreType.DMA((4,))),
        out_specs={0: HBM},
        vmem=12,
    )
    returned = exchange(sent_back, EXPERT).reshape(experts * 24, unit_part)
    chosen = (jnp.arange(experts * 24, dtype=jnp.int32)[:, None] == slot_index).astype(BF16)
    picked = lax.dot_general(chosen, returned, (((0,), (0,)), ((), ())), preferred_element_type=F32)
    picked = picked.reshape(top_count, tokens, unit_part).transpose(1, 0, 2)
    hidden_grad = (gate_prob[:, :, None] * picked).astype(BF16)

    near = jnp.stack([mine, swap_y(mine, 1, y_size)])
    far = swap_y(near, 3, y_size)
    update = call(
        lambda *refs: ortho_kernel(width, *refs),
        jax.ShapeDtypeStruct((1, units, width_part), F32),
        (pair_spots, near, far, swap_core(near), swap_core(far), in_hbm(grad_bf16)),
        (
            pltpu.VMEM((units, units), BF16),
            pltpu.VMEM((dp, units // 2 + 64, 128), BF16),
            pltpu.VMEM((units, width_part), BF16),
            pltpu.VMEM((units, width_part), F32),
            pltpu.SemaphoreType.DMA,
            pltpu.SemaphoreType.DMA((4,)),
        ),
        specs={0: SMEM, 5: HBM},
        out_specs={0: HBM},
        vmem=32,
    )
    return (hidden_grad, update)


def solution(mesh):
    dp, experts = mesh.devices.shape
    x_size = 4
    split = Mesh(
        mesh.devices.reshape(dp // 2, 2, x_size, experts // x_size), ("y", "c", "x", "z")
    )
    rows, cols = ("x", "z"), ("y", "c")
    in_specs = (P(rows, cols), P(rows, None, cols), P(rows, None), P(rows, None), P(rows, None, cols))
    out_specs = (P(rows, None, cols), P(rows, None, cols))
    return jax.shard_map(per_device, mesh=split, in_specs=in_specs, out_specs=out_specs, check_vma=False)
```

```python
import jax
import jax.numpy as jnp
from jax import lax
from jax.experimental import pallas as pl
from jax.experimental.pallas import tpu as pltpu
from jax.sharding import Mesh, PartitionSpec as P

EXPERT = ("x", "z")
MIB = 1024 * 1024
BF16 = jnp.bfloat16
F32 = jnp.float32
SMEM = pl.BlockSpec(memory_space=pltpu.SMEM)
LOOSE = pl.BlockSpec(memory_space=pl.ANY)
HBM = pl.BlockSpec(memory_space=pltpu.HBM)


def shift_y(value, step, size):
    return lax.ppermute(value, "y", [(i, (i + step) % size) for i in range(size)])


def swap_y(value, flip, size):
    return lax.ppermute(value, "y", [(i, i ^ flip) for i in range(size)])


def swap_core(value):
    return lax.ppermute(value, "c", [(0, 1), (1, 0)])


def exchange(value, axes):
    return lax.all_to_all(value, axes, split_axis=0, concat_axis=0, tiled=True)


def nt_dot(left, right):
    return lax.dot_general(left, right, (((1,), (1,)), ((), ())), preferred_element_type=F32)


def nn_dot(left, right):
    return jnp.dot(left, right, preferred_element_type=F32)


def one_hot(rows, index):
    return jnp.where(rows == index, 1.0, 0.0).astype(BF16)


def row_numbers(count):
    return lax.broadcasted_iota(jnp.int32, (count, 1), 0)


def lane_numbers(count):
    return lax.broadcasted_iota(jnp.int32, (1, count), 1)


def send_scaled_kernel(ids_hbm, scaled_ref, out_hbm, main_ref, late_ref, slot_ref, out_ref, ids_ref, sem, sems):
    fetch_ids = pltpu.make_async_copy(ids_hbm, ids_ref, sem)
    fetch_ids.start()
    experts = out_ref.shape[0]
    count, tokens = ids_ref.shape
    earlier = jnp.where(row_numbers(tokens) < lane_numbers(tokens), 1.0, 0.0).astype(BF16)
    passed = jnp.zeros((experts, 1), F32)
    fetch_ids.wait()
    ids, ranks = [], []
    for k in range(count):
        ids.append(ids_ref[k : k + 1, :])
        named = one_hot(row_numbers(experts), ids[k])
        wide = named.astype(F32)
        before = nn_dot(named, earlier) + passed
        ranks.append(jnp.sum(wide * before, axis=0, keepdims=True).astype(jnp.int32))
        passed = passed + jnp.sum(wide, axis=1, keepdims=True)
    expert = jnp.concatenate(ids, axis=1)
    rank = jnp.concatenate(ranks, axis=1)
    late = rank >= 16
    main_index = jnp.where(late, -1, expert * 16 + rank)
    main_ref[...] = main_index
    late_ref[...] = jnp.where(late, expert * 16 + rank - 16, -1)
    slot_ref[...] = expert * 24 + rank
    left_index = jnp.where(late, expert * 8 + rank - 16, -1)
    scaled = scaled_ref[...]
    part = nn_dot(one_hot(row_numbers(experts * 16), main_index), scaled).astype(BF16)
    out_ref[:, 0:16, :] = part.reshape(experts, 16, 128)
    part = nn_dot(one_hot(row_numbers(experts * 8), left_index), scaled)
    out_ref[:, 16:24, :] = part.reshape(experts, 8, 128).astype(BF16)
    store_pieces(out_ref, out_hbm, 4, sems)


def send_grad_kernel(main_ref, late_ref, grad_ref, out_ref):
    experts = out_ref.shape[0]
    tokens, width_part = grad_ref.shape
    blocks = width_part // 128
    grad = grad_ref[...]
    chosen = one_hot(row_numbers(experts * 16), main_ref[...])
    rows = nn_dot(chosen[:, :tokens] + chosen[:, tokens:], grad).astype(BF16)
    for b in range(blocks):
        out_ref[:, 16 * b : 16 * (b + 1), :] = rows[:, b * 128 : (b + 1) * 128].reshape(experts, 16, 128)
    number = row_numbers(experts * 16)
    chosen = one_hot((number & -16) + (number & 3), late_ref[...])
    rows = nn_dot(chosen[:, :tokens] + chosen[:, tokens:], grad)
    column = (number >> 2) & 3
    total = rows[:, 0:128]
    for b in range(1, blocks):
        total = jnp.where(column == b, rows[:, b * 128 : (b + 1) * 128], total)
    out_ref[:, 16 * blocks :, :] = total.astype(BF16).reshape(experts, 16, 128)


def unpack_kernel(got_ref, out_ref):
    experts = got_ref.shape[0]
    out_ref[: experts * 16] = got_ref[:, 0:16, :].reshape(experts * 16, 128)
    tail = got_ref[:, 16:24, :].astype(F32).reshape(experts * 8, 128).astype(BF16)
    number = row_numbers(experts * 4)
    take = one_hot((number >> 2) * 8 + (number & 3), lane_numbers(experts * 8))
    out_ref[experts * 16 :] = nn_dot(take, tail).astype(BF16)


def turn_kernel(spot_ref, own_ref, other_ref, out_ref):
    blocks = out_ref.shape[0] // 128
    y_size = blocks // 2
    for d in range(blocks):
        spot = spot_ref[d]

        @pl.when(spot < y_size)
        def _():
            out_ref[d * 128 : (d + 1) * 128, :] = own_ref[spot].T

        @pl.when(spot >= y_size)
        def _():
            out_ref[d * 128 : (d + 1) * 128, :] = other_ref[spot - y_size].T


def core_kernel(
    spot_ref, got_hbm, weight_hbm, turned_hbm,
    own_ref, other_ref, gradb_hbm,
    rows_ref, got_ref, weight_ref, turned_ref, gradb_ref, sems,
):
    experts = got_ref.shape[0]
    columns = rows_ref.shape[1] // 128
    blocks = weight_ref.shape[0] // 128
    y_size = blocks // 2
    half = blocks // 2
    groups = experts // 16
    part = weight_ref.shape[0] // groups

    def fetch(source, target, size, first):
        copies = []
        for s in range(groups):
            here = slice(s * size, (s + 1) * size)
            copies.append(pltpu.make_async_copy(source.at[here], target.at[here], sems.at[first + s]))
            copies[-1].start()
        return copies

    fetch_got = fetch(got_hbm, got_ref, 16, 0)
    fetch_weight = fetch(weight_hbm, weight_ref, part, groups)

    number = row_numbers(256)
    order = one_hot(((number >> 2) & 15) * 16 + (number >> 6) * 4 + (number & 3), lane_numbers(256))
    for s in range(groups):
        fetch_got[s].wait()
        here = slice(16 * s, 16 * (s + 1))
        late = nn_dot(order, got_ref[here, 16 * columns :, :].reshape(256, 128)).astype(BF16)
        for b in range(columns):
            lanes = slice(b * 128, (b + 1) * 128)
            rows_ref[256 * s : 256 * (s + 1), lanes] = got_ref[here, 16 * b : 16 * (b + 1), :].reshape(256, 128)
            rows_ref[experts * 16 + s * 64 : experts * 16 + (s + 1) * 64, lanes] = late[b * 64 : (b + 1) * 64]
    fetch_turned = fetch(turned_hbm, turned_ref, part, 2 * groups)
    rows = rows_ref[...]
    core = spot_ref[blocks]
    count = rows_ref.shape[0]

    for copy in fetch_weight:
        copy.wait()
    term = nt_dot(rows, weight_ref[...]).astype(BF16)

    def put_terms(own, other):
        for k in range(y_size):
            own_ref[k, :count] = term[:, (2 * k + own) * 128 : (2 * k + own + 1) * 128]
            other_ref[k, :count] = term[:, (2 * k + other) * 128 : (2 * k + other + 1) * 128]

    @pl.when(core == 0)
    def _():
        put_terms(0, 1)

    @pl.when(core != 0)
    def _():
        put_terms(1, 0)

    for copy in fetch_turned:
        copy.wait()
    gradb = nn_dot(turned_ref[...], rows).astype(BF16)
    gradb_ref[...] = gradb
    store_grad = pltpu.make_async_copy(gradb_ref, gradb_hbm, sems.at[3 * groups])
    store_grad.start()
    gram = nt_dot(gradb, gradb).astype(BF16)

    def put_packs(ref, side):
        for n in range(y_size):
            d = 2 * n + side
            i = d % half
            top = i * 128 + (64 if d >= half else 0)
            for k in range(half):
                j = (d + k) % blocks
                ref[n, count + k * 128 : count + (k + 1) * 128, :] = gram[d * 128 : (d + 1) * 128, j * 128 : (j + 1) * 128]
            ref[n, count + half * 128 :, :] = gram[top : top + 64, (i + half) * 128 : (i + half + 1) * 128]

    @pl.when(core == 0)
    def _():
        put_packs(own_ref, 0)
        put_packs(other_ref, 1)

    @pl.when(core != 0)
    def _():
        put_packs(own_ref, 1)
        put_packs(other_ref, 0)

    store_grad.wait()


def add_kernel(own_ref, other_ref, out_ref):
    out_ref[...] = (own_ref[...].astype(F32) + other_ref[...].astype(F32)).astype(BF16)


def store_pieces(source, target, count, sems):
    size = source.shape[0] // count
    copies = []
    for k in range(count):
        piece = slice(k * size, (k + 1) * size)
        copies.append(pltpu.make_async_copy(source.at[piece], target.at[piece], sems.at[k]))
        copies[-1].start()
    for copy in copies:
        copy.wait()


def return_kernel(part_ref, out_hbm, pack_ref, out_ref, sems):
    experts = out_ref.shape[0]
    count = part_ref.shape[1] - pack_ref.shape[0]
    number = row_numbers(128)
    take = one_hot(jnp.where((number & 7) < 4, (number >> 3) * 4 + (number & 7), -1), lane_numbers(64))
    total = part_ref[0].astype(F32)
    for k in range(1, part_ref.shape[0]):
        total = total + part_ref[k].astype(F32)
    total = total.astype(BF16)
    pack_ref[...] = total[count:]
    out_ref[:, 0:16, :] = total[: experts * 16].reshape(experts, 16, 128)
    for s in range(experts // 16):
        left = nn_dot(take, total[experts * 16 + s * 64 : experts * 16 + (s + 1) * 64])
        out_ref[16 * s : 16 * (s + 1), 16:24, :] = left.reshape(16, 8, 128).astype(BF16)
    store_pieces(out_ref, out_hbm, 4, sems)


def ortho_kernel(
    width, spot_ref, own_near_ref, own_far_ref, other_near_ref, other_far_ref, gradb_hbm, out_hbm,
    gram_ref, pack_ref, gradb_ref, out_ref, sem, sems,
):
    fetch_grad = pltpu.make_async_copy(gradb_hbm, gradb_ref, sem)
    fetch_grad.start()
    blocks = gram_ref.shape[0] // 128
    half = blocks // 2
    squares = jnp.zeros((8, 128), F32)
    for i, ref in enumerate((own_near_ref, own_far_ref, other_near_ref, other_far_ref)):
        for k in range(2):
            pack = ref[k]
            pack_ref[2 * i + k] = pack
            square = pack.astype(F32)
            square = square * square
            squares = squares + 2.0 * jnp.sum(square.reshape(-1, 8, 128), axis=0)
            squares = squares - jnp.sum(square[:128].reshape(-1, 8, 128), axis=0)
    norm_sq = jnp.sqrt(jnp.sum(squares, keepdims=True)) + 1e-06
    for d in range(blocks):
        spot = spot_ref[d]
        rows = slice(d * 128, (d + 1) * 128)
        for k in range(half):
            lanes = slice((d + k) % blocks * 128, ((d + k) % blocks + 1) * 128)
            block = pack_ref[spot, k * 128 : (k + 1) * 128, :]
            gram_ref[rows, lanes] = block
            if k > 0:
                gram_ref[lanes, rows] = block.T
        i = d % half
        top = i * 128 + (64 if d >= half else 0)
        gram_ref[top : top + 64, (i + half) * 128 : (i + half + 1) * 128] = pack_ref[spot, half * 128 :, :]
    for i in range(half):
        upper = gram_ref[i * 128 : (i + 1) * 128, (i + half) * 128 : (i + half + 1) * 128]
        gram_ref[(i + half) * 128 : (i + half + 1) * 128, i * 128 : (i + 1) * 128] = upper.T

    inverse = 1.0 / norm_sq
    gram = gram_ref[...]
    fetch_grad.wait()
    first = (gradb_ref[...].astype(F32) * lax.rsqrt(norm_sq)).astype(BF16)

    def apply(value):
        return nn_dot(gram, value) * inverse

    second = (1.5 * first.astype(F32) - 0.5 * apply(first)).astype(BF16)
    power_one = apply(second).astype(BF16)
    power_two = apply(power_one).astype(BF16)
    near_terms = 1.5 * second.astype(F32) - 0.5 * (2.25 * power_one.astype(F32) - 1.5 * power_two.astype(F32))
    size = gram.shape[0] // 2
    part = size // 2
    stores = []
    for h in range(2):
        rows = slice(h * size, (h + 1) * size)
        power_three = nn_dot(gram[rows], power_two) * inverse
        out_ref[rows] = (near_terms[rows] - 0.125 * power_three) * width**0.5
        for q in range(2):
            piece = slice(h * size + q * part, h * size + (q + 1) * part)
            stores.append(pltpu.make_async_copy(out_ref.at[piece], out_hbm.at[0, piece], sems.at[2 * h + q]))
            stores[-1].start()
    for copy in stores:
        copy.wait()


def in_hbm(value):
    return pltpu.with_memory_space_constraint(value, pltpu.HBM)


def whole(value):
    return pl.BlockSpec(value.shape, lambda *_: (0,) * len(value.shape))


def call(kernel, outs, ins, scratch=(), vmem=24, steps=(), specs=None, out_specs=None):
    specs = specs or {}
    out_specs = out_specs or {}
    flat, tree = jax.tree.flatten(outs)
    return pl.pallas_call(
        kernel,
        out_shape=outs,
        grid=steps,
        in_specs=[specs.get(i, whole(value)) for i, value in enumerate(ins)],
        out_specs=jax.tree.unflatten(tree, [out_specs.get(i, whole(value)) for i, value in enumerate(flat)]),
        scratch_shapes=list(scratch),
        compiler_params=pltpu.CompilerParams(vmem_limit_bytes=vmem * MIB),
    )(*ins)


def per_device(grad_out, hidden, gate_prob, expert_ids, weights):
    tokens, width_part = grad_out.shape
    top_count = expert_ids.shape[1]
    unit_part = hidden.shape[2]
    units = weights.shape[1]
    experts = lax.axis_size("x") * lax.axis_size("z")
    y_size = lax.axis_size("y")
    dp = y_size * 2
    width = width_part * dp
    capacity = 5 * tokens * top_count // (4 * experts)
    total_slots = experts * capacity
    pair_count = tokens * top_count
    y = lax.axis_index("y")
    c = lax.axis_index("c")
    block = jnp.arange(dp, dtype=jnp.int32)
    other_core = (block % 2) ^ c
    flip = y ^ (block // 2)
    pair_spot = other_core * y_size + (flip ^ (flip >> 1))
    came_from = other_core * y_size + (y - block // 2) % y_size
    core = jnp.full((1,), c)
    pair_spots = jnp.concatenate([pair_spot, core]).astype(jnp.int32)

    scaled_part = (gate_prob[:, :, None] * hidden.astype(F32)).astype(BF16)
    scaled_part = scaled_part.transpose(1, 0, 2).reshape(pair_count, unit_part)
    columns = width_part // 128

    def shape(*dims):
        return jax.ShapeDtypeStruct(dims, BF16)

    row = jax.ShapeDtypeStruct((1, pair_count), jnp.int32)
    sent_scaled, main_index, late_index, slot_index = call(
        send_scaled_kernel,
        (pltpu.HBM((experts, 24, 128), BF16), row, row, row),
        (in_hbm(expert_ids.T), scaled_part),
        (
            pltpu.VMEM((experts, 24, 128), BF16),
            pltpu.VMEM((top_count, tokens), jnp.int32),
            pltpu.SemaphoreType.DMA,
            pltpu.SemaphoreType.DMA((4,)),
        ),
        specs={0: HBM},
        out_specs={0: HBM},
    )
    got_scaled = exchange(sent_scaled, EXPERT)
    got = exchange(
        call(send_grad_kernel, shape(experts, 20 * columns, 128), (main_index, late_index, grad_out)), EXPERT
    )

    scaled = call(unpack_kernel, shape(total_slots, unit_part), (got_scaled,), vmem=8)
    gathered = jnp.stack([scaled] + [shift_y(scaled, k, y_size) for k in range(1, y_size)])
    turned = call(
        turn_kernel, pltpu.HBM((units, total_slots), BF16), (came_from.astype(jnp.int32), gathered, swap_core(gathered)),
        specs={0: SMEM},
        vmem=20,
    )

    pack_rows = units // 2 + 64
    dp_parts = shape(y_size, total_slots + pack_rows, 128)
    groups = experts // 16
    own, other, grad_bf16 = call(
        core_kernel,
        (dp_parts, dp_parts, pltpu.HBM((units, width_part), BF16)),
        (pair_spots, in_hbm(got), in_hbm(weights[0]), in_hbm(turned)),
        (
            pltpu.VMEM((total_slots, width_part), BF16),
            pltpu.VMEM(got.shape, BF16),
            pltpu.VMEM((units, width_part), BF16),
            pltpu.VMEM((units, total_slots), BF16),
            pltpu.VMEM((units, width_part), BF16),
            pltpu.SemaphoreType.DMA((3 * groups + 1,)),
        ),
        specs={0: SMEM, 1: HBM, 2: HBM, 3: HBM},
        out_specs={2: HBM},
        vmem=32,
    )
    both = call(add_kernel, dp_parts, (own, swap_core(other)), vmem=12)
    parts = exchange(both, "y")
    sent_back, mine = call(
        return_kernel,
        (pltpu.HBM((experts, 24, 128), BF16), shape(pack_rows, 128)),
        (parts,),
        (pltpu.VMEM((experts, 24, 128), BF16), pltpu.SemaphoreType.DMA((4,))),
        out_specs={0: HBM},
        vmem=12,
    )
    returned = exchange(sent_back, EXPERT).reshape(experts * 24, unit_part)
    chosen = (jnp.arange(experts * 24, dtype=jnp.int32)[:, None] == slot_index).astype(BF16)
    picked = lax.dot_general(chosen, returned, (((0,), (0,)), ((), ())), preferred_element_type=F32)
    picked = picked.reshape(top_count, tokens, unit_part).transpose(1, 0, 2)
    hidden_grad = (gate_prob[:, :, None] * picked).astype(BF16)

    near = jnp.stack([mine, swap_y(mine, 1, y_size)])
    far = swap_y(near, 3, y_size)
    update = call(
        lambda *refs: ortho_kernel(width, *refs),
        jax.ShapeDtypeStruct((1, units, width_part), F32),
        (pair_spots, near, far, swap_core(near), swap_core(far), in_hbm(grad_bf16)),
        (
            pltpu.VMEM((units, units), BF16),
            pltpu.VMEM((dp, units // 2 + 64, 128), BF16),
            pltpu.VMEM((units, width_part), BF16),
            pltpu.VMEM((units, width_part), F32),
            pltpu.SemaphoreType.DMA,
            pltpu.SemaphoreType.DMA((4,)),
        ),
        specs={0: SMEM, 5: HBM},
        out_specs={0: HBM},
        vmem=32,
    )
    return (hidden_grad, update)


def solution(mesh):
    dp, experts = mesh.devices.shape
    x_size = 4
    split = Mesh(
        mesh.devices.reshape(dp // 2, 2, x_size, experts // x_size), ("y", "c", "x", "z")
    )
    rows, cols = ("x", "z"), ("y", "c")
    in_specs = (P(rows, cols), P(rows, None, cols), P(rows, None), P(rows, None), P(rows, None, cols))
    out_specs = (P(rows, None, cols), P(rows, None, cols))
    return jax.shard_map(per_device, mesh=split, in_specs=in_specs, out_specs=out_specs, check_vma=False)
```
